512 devices in a mesh: req: 64 (over z, x), head: 8 (over y, core).
Axes of the slice: x: 4, y: 4, z: 16, core: 2. Of those that a mesh axis runs over, the one named last changes fastest.
Arguments:
- tokens: bfloat16 [64, 512, 1024], P('req', 'head'), may hold values from -6 to 6
- gain: bfloat16 [1024], replicated, may hold values from 0.099609375 to 1.8984375
- projection_weight: bfloat16 [1024, 4, 1024], P(None, None, 'head'), may hold values from -0.1875 to 0.1875
- output_weight: bfloat16 [1024, 1024], P('head'), may hold values from -0.1875 to 0.1875
- persist: bfloat16 [2, 16, 1024], P(None, None, 'head'), may hold values from -6 to 6
- cache_page_slots: bfloat16 [64, 64, 64, 2, 1024], P('req', None, None, None, 'head'), may hold values from -250 to 250
- cached_length: int32 [64], P('req'), may hold values from 33 to 4096, as said below
- page_keeper: int32 [64, 128], P('req'), may hold values from -1 to 63, as said below
- page_slot_index: int32 [64, 128], P('req'), may hold values from -1 to 1, as said below
- memory_state: float32 [2, 64, 8, 128, 128], P(None, 'req', 'head'), may hold values from -3 to 3
- retention: float32 [64, 8], P('req', 'head'), may hold values from 0.2 to 1
- momentum: float32 [64, 8], P('req', 'head'), may hold values from 0.2 to 0.9
- memory_step_scale: float32 [64, 8], P('req', 'head'), may hold values from 0.02 to 0.3
- halving_updates: int32 [64, 8], P('req'), may hold values 0 or 1
Outputs:
- layer_out: bfloat16 [64, 512, 1024], P('req', 'head')
- new_state: float32 [2, 64, 8, 128, 128], P(None, 'req', 'head')
The draws below stay inside these ranges and needn't reach their ends.
Inputs may be any that keep to these rules, and one draw needn't show every extreme that they name: `cached_length`: the requests of one device hold together at most 128 pages. `page_keeper`: pages j below cached_length[r] / 32 (rounded up) have a keeper; later entries are -1. No keeper and slot serve two pages of the requests of one device. `page_slot_index`: -1 exactly where page_keeper is -1.
All inputs are finite; a program needn't handle non-finite values. No bound on the sum of `halving_updates` on one device may be relied on, other than what follows from the above.
Results may differ from the reference program's by a relative error of at most 0.012.
The reference program's roundings to bfloat16 on the way count: a program that leaves them out, or rounds other values in their place, can miss the bound.
Values may be sent and summed in bfloat16 or wider, within the bound.
A program may use at most 64 MiB of HBM per device.

```python
import math
import jax
import jax.numpy as jnp
from jax import lax

D = 1024
H = 8
HD = 128
PERSIST = 16
BLK = 64
PREFILL = 512
PAGE = 32
REQ_DEV = 1
REQUEST_TOTAL = 64
MAXPAGES = 128
CAP = 2
UPDATE_BLOCKS = 8
N_HEAD = 8


def layout_tables(key):
    base = jax.random.fold_in(key, 7)
    first, second, third, fourth = jax.random.split(base, 4)
    homes = REQUEST_TOTAL // REQ_DEV
    bound = MAXPAGES + (REQ_DEV - 1) * (MAXPAGES // 2)
    raw_pages = jax.random.randint(first, (homes, REQ_DEV), CAP, MAXPAGES + 1)
    columns_list = []
    running = jnp.zeros((homes,), jnp.int32)
    for which in range(REQ_DEV):
        room = bound - running - (REQ_DEV - 1 - which) * CAP
        taken = jnp.minimum(raw_pages[:, which], room).astype(jnp.int32)
        columns_list.append(taken)
        running = running + taken
    pages = jnp.stack(columns_list, axis=1)
    chosen = jax.random.randint(second, (), 0, homes)
    forced = jnp.where(jnp.arange(REQ_DEV) == 0, MAXPAGES, MAXPAGES // 2).astype(jnp.int32)
    is_chosen = jnp.arange(homes)[:, None] == chosen
    pages = jnp.where(is_chosen, forced[None, :], pages)
    trims = jax.random.randint(third, (homes, REQ_DEV), 0, PAGE)
    trims = jnp.where(is_chosen & (jnp.arange(REQ_DEV)[None, :] == 0), 0, trims)
    lengths = (pages * PAGE - trims).reshape(REQUEST_TOTAL).astype(jnp.int32)
    before = jnp.cumsum(pages, axis=1) - pages
    keepers = jax.vmap(lambda single: jax.random.permutation(single, homes))(jax.random.split(fourth, homes))
    page_ids = jnp.arange(MAXPAGES)
    slot = before[:, :, None] + page_ids[None, None, :]
    used = page_ids[None, None, :] < pages[:, :, None]
    owners = jnp.take_along_axis(keepers, (slot % homes).reshape(homes, REQ_DEV * MAXPAGES), axis=1).reshape(homes, REQ_DEV, MAXPAGES)
    owners = jnp.where(used, owners, -1).reshape(REQUEST_TOTAL, MAXPAGES).astype(jnp.int32)
    lanes = jnp.where(used, slot // homes, -1).reshape(REQUEST_TOTAL, MAXPAGES).astype(jnp.int32)
    return (lengths, owners, lanes)


def draw_cached_length(key, part):
    return layout_tables(key)[0]


def draw_page_keeper(key, part):
    return layout_tables(key)[1]


def draw_page_slot_index(key, part):
    return layout_tables(key)[2]


def draw_cache_page_slots(key, part):
    homes = REQUEST_TOTAL // REQ_DEV
    span = CAP * PAGE
    shape = (homes, homes, span // 2, 2, 2, H * HD)
    first, second = jax.random.split(key, 2)
    base = jnp.clip(1.5 * jax.random.normal(first, shape, jnp.float32), -6.0, 6.0)
    chosen = jax.random.randint(second, (homes, homes, span // 2), 0, 1024) == 0
    lead_key = base[:, :, :, 0, 0, :]
    boosted = jnp.stack([40.0 * lead_key, 40.4 * lead_key], axis=3)
    keys_new = jnp.where(chosen[:, :, :, None, None], boosted, base[:, :, :, :, 0, :])
    result = jnp.stack([keys_new, base[:, :, :, :, 1, :]], axis=4).reshape(homes, homes, span, 2, H * HD)
    return result.astype(jnp.bfloat16)


def set_ends(array, own_key, low, top_value):
    longest = array.shape.index(max(array.shape))
    spots = []
    for shift in (0, 1):
        where = [jax.random.randint(jax.random.fold_in(own_key, axis), (), 0, length) for axis, length in enumerate(array.shape)]
        where[longest] = (where[longest] + shift) % array.shape[longest]
        spots.append(tuple(where))
    return array.at[spots[0]].set(low).at[spots[1]].set(top_value)


def steps_of(rng, dims, pieces, smallest, largest):
    level = 1.0
    for dim, parts in pieces:
        draws = jax.random.uniform(jax.random.fold_in(jax.random.fold_in(rng, 6), dim), (parts,), jnp.float32, smallest / len(pieces), largest / len(pieces))
        level = level * jnp.repeat(jnp.exp(draws), dims[dim] // parts).reshape((-1,) + (1,) * (len(dims) - 1 - dim))
    return level


def scatter_about(own_key, dims, deviation, most, pieces=(), kind=jnp.bfloat16):
    array = jax.random.normal(own_key, dims, jnp.float32) * deviation
    if len(pieces) > 0:
        array = steps_of(own_key, dims, pieces, -0.22, 0.18) * array
    return jnp.clip(array, min=-most, max=most).astype(kind)


def setup_inputs(seed: int = 0) -> dict:
    splits = jax.random.split(jax.random.key(seed), 15)
    tokens = scatter_about(splits[0], (REQUEST_TOTAL, PREFILL, D), 1.0, 6.0, ((0, 64), (1, 8)))
    gain = jnp.clip(1.0 + 0.18 * jax.random.normal(splits[1], (D,), jnp.float32), 0.099609375, 1.8984375).astype(jnp.bfloat16)
    projection_weight = scatter_about(splits[2], (D, 4, H * HD), D ** -0.5, 0.1875, ((2, 8),))
    output_weight = scatter_about(splits[3], (H * HD, D), (H * HD) ** -0.5, 0.1875, ((0, 8),))
    persist = scatter_about(splits[4], (2, PERSIST, H * HD), 1.0, 6.0, ((2, 8),))
    cache_page_slots = draw_cache_page_slots(jax.random.fold_in(splits[14], 71), 0)
    cached_length = draw_cached_length(jax.random.fold_in(splits[14], 71), 0)
    page_keeper = draw_page_keeper(jax.random.fold_in(splits[14], 71), 0)
    page_slot_index = draw_page_slot_index(jax.random.fold_in(splits[14], 71), 0)
    memory_state = scatter_about(splits[9], (2, REQUEST_TOTAL, H, HD, HD), 0.5, 3.0, ((1, 64), (2, 8)), jnp.float32)
    retention = jnp.clip(jnp.exp(math.log(1.0) - 1.609438 * jax.random.uniform(splits[10], (REQUEST_TOTAL, H), jnp.float32) ** steps_of(splits[10], (REQUEST_TOTAL, H), ((0, 64), (1, 8)), -0.2, 0.2)), 0.2, 1.0)
    momentum = jnp.clip(0.2 + 0.7 * jax.random.uniform(splits[11], (REQUEST_TOTAL, H), jnp.float32) ** steps_of(splits[11], (REQUEST_TOTAL, H), ((0, 64), (1, 8)), -0.2, 0.2), 0.2, 0.9)
    memory_step_scale = jnp.clip(jnp.exp(math.log(0.3) - 2.7080503 * jax.random.uniform(splits[12], (REQUEST_TOTAL, H), jnp.float32) ** steps_of(splits[12], (REQUEST_TOTAL, H), ((0, 64), (1, 8)), -0.2, 0.2)), 0.02, 0.3)
    halving_updates = set_ends((jax.random.randint(splits[13], (REQUEST_TOTAL, UPDATE_BLOCKS), 0, 4) < 1).astype(jnp.int32), jax.random.fold_in(splits[13], 1), 0, 1)
    return dict(tokens=tokens, gain=gain, projection_weight=projection_weight, output_weight=output_weight, persist=persist, cache_page_slots=cache_page_slots, cached_length=cached_length, page_keeper=page_keeper, page_slot_index=page_slot_index, memory_state=memory_state, retention=retention, momentum=momentum, memory_step_scale=memory_step_scale, halving_updates=halving_updates)


norm_eps = 1e-05
unit_eps = 1e-06

def unit_rows(values_f):
    return values_f * lax.rsqrt(lax.optimization_barrier(jnp.sum(values_f * values_f, axis=-1, keepdims=True)) + unit_eps)

def reference(tokens, gain, projection_weight, output_weight, persist, cache_page_slots, cached_length, page_keeper, page_slot_index, memory_state, retention, momentum, memory_step_scale, halving_updates):
    columns = H * HD
    homes = REQUEST_TOTAL // REQ_DEV
    scale = 1.0 / math.sqrt(HD)
    highest = lax.Precision.HIGHEST
    flat_w = projection_weight.reshape(D, 4 * columns)
    gain_f = gain.astype(jnp.float32)
    causal = jnp.arange(PREFILL)[:, None] >= jnp.arange(PREFILL)[None, :]
    slot_ids = jnp.arange(homes * CAP, dtype=jnp.int32)
    page_ids = jnp.arange(MAXPAGES, dtype=jnp.int32)
    position = jnp.arange(PAGE, dtype=jnp.int32)
    group_w = output_weight.reshape(N_HEAD, columns // N_HEAD, D).astype(jnp.float32)
    persist_keys = persist[0].reshape(PERSIST, H, HD).astype(jnp.float32)
    persist_values = persist[1].reshape(PERSIST, H, HD).astype(jnp.float32)

    def one_request(index_value):
        inputs = tokens[index_value].astype(jnp.float32)
        normed = (inputs * lax.rsqrt(lax.optimization_barrier(jnp.mean(inputs * inputs, axis=-1, keepdims=True)) + norm_eps) * gain_f).astype(jnp.bfloat16)
        projected = jnp.dot(normed, flat_w, preferred_element_type=jnp.float32).reshape(PREFILL, 4, H, HD)
        rounded = (projected[:, 0].astype(jnp.bfloat16), projected[:, 1].astype(jnp.bfloat16), projected[:, 2].astype(jnp.bfloat16))
        rounded = lax.optimization_barrier(rounded)
        queries = rounded[0].astype(jnp.float32)
        own_keys = rounded[1].astype(jnp.float32)
        own_values = rounded[2].astype(jnp.float32)
        gate = projected[:, 3]
        pool = lax.dynamic_index_in_dim(cache_page_slots, index_value // REQ_DEV, axis=1, keepdims=False)
        cache_keys = pool[:, :, 0].reshape(homes * CAP * PAGE, H, HD).astype(jnp.float32)
        cache_values = pool[:, :, 1].reshape(homes * CAP * PAGE, H, HD).astype(jnp.float32)
        filled = jnp.clip(cached_length[index_value] - page_ids * PAGE, 0, PAGE)
        slot_of = page_keeper[index_value] * CAP + page_slot_index[index_value]
        slot_fill = lax.optimization_barrier(jnp.sum(jnp.where(slot_of[:, None] == slot_ids[None, :], filled[:, None], 0), axis=0))
        valid = (position[None, :] < slot_fill[:, None]).reshape(homes * CAP * PAGE)
        score_p = jnp.einsum('thc,khc->thk', queries, persist_keys) * scale
        score_c = jnp.where(valid[None, None, :], jnp.einsum('thc,khc->thk', queries, cache_keys) * scale, -jnp.inf)
        score_t = jnp.where(causal[:, None, :], jnp.einsum('thc,khc->thk', queries, own_keys) * scale, -jnp.inf)
        row_max = jnp.maximum(jnp.maximum(lax.optimization_barrier(jnp.max(score_p, axis=-1, keepdims=True)), lax.optimization_barrier(jnp.max(score_c, axis=-1, keepdims=True))), lax.optimization_barrier(jnp.max(score_t, axis=-1, keepdims=True)))
        exp_p = jnp.exp(score_p - row_max)
        exp_c = jnp.exp(score_c - row_max)
        exp_t = jnp.exp(score_t - row_max)
        total = lax.optimization_barrier(jnp.sum(exp_p, axis=-1, keepdims=True)) + lax.optimization_barrier(jnp.sum(exp_c, axis=-1, keepdims=True)) + lax.optimization_barrier(jnp.sum(exp_t, axis=-1, keepdims=True))
        weight_set = lax.optimization_barrier((exp_p.astype(jnp.bfloat16), exp_c.astype(jnp.bfloat16), exp_t.astype(jnp.bfloat16)))
        mixed = jnp.einsum('thk,khc->thc', weight_set[0].astype(jnp.float32), persist_values)
        mixed = mixed + jnp.einsum('thk,khc->thc', weight_set[1].astype(jnp.float32), cache_values)
        mixed = mixed + jnp.einsum('thk,khc->thc', weight_set[2].astype(jnp.float32), own_values)
        attended = mixed / total
        unit_attn = attended * lax.rsqrt(lax.optimization_barrier(jnp.mean(attended * attended, axis=-1, keepdims=True)) + unit_eps)
        query_unit = unit_rows(queries)
        key_unit = unit_rows(own_keys)
        state_m = memory_state[0, index_value]
        state_s = memory_state[1, index_value]
        rate_values = retention[index_value]
        pushes = momentum[index_value]
        strides = memory_step_scale[index_value]
        reads = []
        for block_span in range(UPDATE_BLOCKS):
            lower = block_span * BLK
            q_block = query_unit[lower:lower + BLK]
            k_block = key_unit[lower:lower + BLK]
            v_block = own_values[lower:lower + BLK]
            reads.append(jnp.einsum('thc,hdc->thd', q_block, state_m, precision=highest))
            errors = jnp.einsum('thc,hdc->thd', k_block, state_m, precision=highest) - v_block
            grads = jnp.einsum('thd,thc->hdc', errors, k_block, precision=highest)
            state_s = pushes[:, None, None] * state_s - strides[:, None, None] * grads
            keeper_list = rate_values * jnp.where(halving_updates[index_value, block_span] == 1, 0.5, 1.0)
            state_m = keeper_list[:, None, None] * state_m + state_s
        memory_read = jnp.concatenate(reads, axis=0)
        head_out = (unit_attn + jax.nn.sigmoid(gate) * memory_read).astype(jnp.bfloat16)
        head_out = lax.optimization_barrier(head_out)
        grouped = head_out.reshape(PREFILL, N_HEAD, columns // N_HEAD).astype(jnp.float32)
        partials = jnp.einsum('tgc,gcd->tgd', grouped, group_w).astype(jnp.bfloat16)
        partials = lax.optimization_barrier(partials)
        layer_out = lax.optimization_barrier(jnp.sum(partials.astype(jnp.float32), axis=1)).astype(jnp.bfloat16)
        return (layer_out, jnp.stack([state_m, state_s]))
    outputs, states = lax.map(one_request, jnp.arange(REQUEST_TOTAL, dtype=jnp.int32))
    return (outputs, jnp.transpose(states, (1, 0, 2, 3, 4)))
```

```python
import functools
import math

import jax
import jax.numpy as jnp
from jax import lax
from jax.experimental import pallas as pl
from jax.experimental.pallas import tpu as pltpu
from jax.sharding import PartitionSpec as P

HD = 128
BLK = 64
PAGE = 32
NX = 4
CORES = 2
MESH = pl.DeviceIdType.MESH
NEG = -1e30
FLOOR = -5e29
NORM_EPS = 1e-05
UNIT_EPS = 1e-06
HIGHEST = lax.Precision.HIGHEST


def mm(left, right):
    return jnp.dot(left, right, preferred_element_type=jnp.float32)


def exact(left, right):
    return jnp.dot(left, right, precision=HIGHEST, preferred_element_type=jnp.float32)


def soften(scores):
    top = jnp.maximum(jnp.max(scores, axis=0, keepdims=True), FLOOR)
    grown = jnp.exp(scores - top)
    return top, jnp.sum(grown, axis=0, keepdims=True), grown.astype(jnp.bfloat16)


def kernel(
    nz,
    ny,
    tokens_ref,
    gain_ref,
    weight_ref,
    out_weight_ref,
    persist_ref,
    cache_ref,
    length_ref,
    keeper_ref,
    slot_ref,
    state_ref,
    retention_ref,
    momentum_ref,
    stride_ref,
    halving_ref,
    layer_ref,
    new_state_ref,
    tok_buf,
    wout_buf,
    wide,
    w_parts,
    normed,
    kv_buf,
    q_own,
    q_buf,
    fill_own,
    fill_buf,
    keys_own,
    values_t,
    key_unit,
    key_unit_t,
    query_unit_t,
    gate_t,
    read_t,
    mem_m,
    mem_s,
    kv_wide,
    part_acc,
    part_ml,
    send_acc,
    send_ml,
    recv_acc,
    recv_ml,
    home_acc,
    home_ml,
    hout_buf,
    hrecv,
    tok_send,
    tok_recv,
    wo_send,
    wo_recv,
    kv_send,
    kv_recv,
    kv_local,
    q_send,
    q_recv,
    f_send,
    f_recv,
    a_send,
    a_recv,
    m_send,
    m_recv,
    h_send,
    h_recv,
):
    req = lax.axis_index("req")
    head = lax.axis_index("head")
    z, x = req // NX, lax.rem(req, NX)
    y, core = head // CORES, lax.rem(head, CORES)
    heads = ny * CORES
    rows = tokens_ref.shape[0]
    prefill = heads * rows
    half = prefill // 2
    width = tokens_ref.shape[1]
    span = cache_ref.shape[1]
    plane = NX * span // 2
    depth = nz // 2
    scale = 1.0 / math.sqrt(HD)

    partner = y * CORES + (1 - core)
    right_head = lax.rem(y + 1, ny) * CORES + core
    left_head = lax.rem(y + ny - 1, ny) * CORES + core
    anti_head = lax.rem(y + 2, ny) * CORES + core
    z_next = (lax.rem(z + 1, nz) * NX + x, head)
    z_back = (lax.rem(z + nz - 1, nz) * NX + x, head)
    ahead = (z_next, z_back)

    barrier = pltpu.get_barrier_semaphore()
    for peer in ahead:
        pl.semaphore_signal(barrier, inc=1, device_id=peer, device_id_type=MESH)
    for j in range(1, NX):
        peer = (z * NX + lax.rem(x + j, NX), head)
        pl.semaphore_signal(barrier, inc=1, device_id=peer, device_id_type=MESH)
    for j in range(1, heads):
        peer = (req, lax.rem(head + j, heads))
        pl.semaphore_signal(barrier, inc=1, device_id=peer, device_id_type=MESH)
    pl.semaphore_wait(barrier, 2 + NX - 1 + heads - 1)

    def remote(src, dst, send, recv, device):
        return pltpu.make_async_remote_copy(
            src_ref=src,
            dst_ref=dst,
            send_sem=send,
            recv_sem=recv,
            device_id=device,
            device_id_type=MESH,
        )

    def spread(own, buf, send, recv):
        cut = own.shape[0] // 2
        low, high = pl.ds(0, cut), pl.ds(cut, cut)
        to = lambda src, dst, i, k, g: remote(src, dst, send.at[i], recv.at[k], (req, g))
        from_left = buf.at[left_head]
        from_right = buf.at[right_head]
        return (
            to(own, buf.at[head], 0, 0, partner),
            to(own, buf.at[head], 1, 1, right_head),
            to(own, buf.at[head], 2, 2, left_head),
            to(buf.at[left_head, low], buf.at[left_head, low], 3, 3, right_head),
            to(from_left, from_left, 4, 5, partner),
            to(buf.at[right_head, high], buf.at[right_head, high], 5, 4, left_head),
            to(from_right, from_right, 6, 6, partner),
            to(buf.at[anti_head], buf.at[anti_head], 7, 7, partner),
        )

    def spread_mid(c):
        c[1].wait_recv()
        c[3].start()
        c[4].start()
        c[2].wait_recv()
        c[5].start()
        c[6].start()

    def spread_late(c):
        c[3].wait_recv()
        c[5].wait_recv()
        c[7].start()

    tok = spread(tokens_ref, tok_buf, tok_send, tok_recv)
    wout = spread(out_weight_ref, wout_buf, wo_send, wo_recv)
    for c in tok[:3]:
        c.start()

    def kv_copy(rel, j):
        to_x = lax.rem(x + j, NX)
        return remote(
            cache_ref.at[lax.rem(z + rel, nz) * NX + to_x],
            kv_buf.at[rel, x],
            kv_send.at[rel, j - 1],
            kv_recv.at[rel, j - 1],
            (z * NX + to_x, head),
        )

    def kv_stay(rel):
        return pltpu.make_async_copy(
            cache_ref.at[lax.rem(z + rel, nz) * NX + x], kv_buf.at[rel, x], kv_local.at[rel]
        )

    def kv_begin(i, carry):
        sign = 2 * lax.rem(i, 2) - 1
        rel = lax.rem(nz + ((i + 1) // 2) * sign, nz)
        kv_stay(rel).start()
        for j in range(1, NX):
            kv_copy(rel, j).start()
        return carry

    lax.fori_loop(0, nz, kv_begin, 0)

    wide[...] = weight_ref[...].astype(jnp.float32)
    for part in range(4):
        w_parts[part] = wide[pl.ds(part, width, stride=4), :].astype(jnp.bfloat16)

    ids = lax.broadcasted_iota(jnp.int32, (1, 128), 1)
    filled = jnp.clip(length_ref[0] - ids * PAGE, 0, PAGE)
    slot_of = keeper_ref[...] * 2 + slot_ref[...]
    filled_t = jnp.transpose(jnp.broadcast_to(filled.astype(jnp.float32), (128, 128)))
    slot_t = jnp.transpose(jnp.broadcast_to(slot_of.astype(jnp.float32), (128, 128)))
    lanes_f = lax.broadcasted_iota(jnp.int32, (128, 128), 1).astype(jnp.float32)
    slot_fill = jnp.sum(jnp.where(slot_t == lanes_f, filled_t, 0.0), axis=0, keepdims=True)
    fill_own[...] = jnp.broadcast_to(slot_fill, (8, 128))

    def norm_block(block, g):
        x_f = block.astype(jnp.float32)
        mean = jnp.mean(x_f * x_f, axis=-1, keepdims=True)
        scaled = x_f * lax.rsqrt(mean + NORM_EPS) * gain_ref[...].astype(jnp.float32)
        normed[pl.ds(pl.multiple_of(g * rows, rows), rows), :] = scaled.astype(jnp.bfloat16)

    norm_block(tokens_ref[...], head)
    spread_mid(tok)
    tok[0].wait_recv()
    norm_block(tok_buf[partner], partner)
    norm_block(tok_buf[left_head], left_head)
    norm_block(tok_buf[right_head], right_head)
    tok[4].wait_recv()
    flip = lambda g: (g // CORES) * CORES + (1 - core)
    norm_block(tok_buf[flip(left_head)], flip(left_head))
    tok[6].wait_recv()
    norm_block(tok_buf[flip(right_head)], flip(right_head))
    spread_late(tok)
    for c in wout[:3]:
        c.start()
    norm_block(tok_buf[anti_head], anti_head)
    tok[7].wait_recv()
    norm_block(tok_buf[flip(anti_head)], flip(anti_head))

    q_t = jnp.transpose(mm(normed[...], w_parts[0]))
    for h in range(2):
        q_own[h] = q_t[:, h * half : (h + 1) * half].astype(jnp.bfloat16)

    def q_copy(d, h, k):
        src = q_own.at[h] if isinstance(k, int) and k == 0 else q_buf.at[d, k - 1, h]
        return remote(
            src, q_buf.at[d, k, h], q_send.at[d, h, k], q_recv.at[d, h, k], ahead[d]
        )

    def q_done(d, h, k):
        place = q_buf.at[d, k, h]
        return remote(place, place, q_send.at[d, h, k], q_recv.at[d, h, k], ahead[d])

    def f_done(d, k):
        place = fill_buf.at[d, k]
        return remote(place, place, f_send.at[d, k], f_recv.at[d, k], ahead[d])

    def f_copy(d, k):
        src = fill_own if isinstance(k, int) and k == 0 else fill_buf.at[d, k - 1]
        return remote(src, fill_buf.at[d, k], f_send.at[d, k], f_recv.at[d, k], ahead[d])

    for d in range(2):
        f_copy(d, 0).start()
        for h in (d, 1 - d):
            q_copy(d, h, 0).start()

    def unit_columns(v):
        return v * lax.rsqrt(jnp.sum(v * v, axis=0, keepdims=True) + UNIT_EPS)

    for h in range(2):
        query_unit_t[h] = unit_columns(q_own[h].astype(jnp.float32))
    k_bf = mm(normed[...], w_parts[1]).astype(jnp.bfloat16)
    keys_own[...] = k_bf
    k_f = k_bf.astype(jnp.float32)
    k_unit = k_f * lax.rsqrt(jnp.sum(k_f * k_f, axis=-1, keepdims=True) + UNIT_EPS)
    v_bf = mm(normed[...], w_parts[2]).astype(jnp.bfloat16)
    v_t = jnp.transpose(v_bf.astype(jnp.float32))
    k_unit_t = jnp.transpose(k_unit)
    gates = jnp.transpose(mm(normed[...], w_parts[3]))
    values_t[...] = v_t.astype(jnp.bfloat16)
    for b in range(prefill // BLK):
        columns = slice(b * BLK, (b + 1) * BLK)
        key_unit[b] = k_unit[columns, :]
        key_unit_t[b] = jnp.concatenate([k_unit_t[:, columns], v_t[:, columns]], axis=1)
    for h in range(2):
        gate_t[h] = gates[:, h * half : (h + 1) * half]
    mem_m[...] = state_ref[0]
    mem_s[...] = state_ref[1]

    def split_kv(rel):
        kv_stay(rel).wait()
        for j in range(1, NX):
            kv_copy(rel, j).wait_recv()
        for s in range(NX):
            kv_wide[pl.ds(s * span, span), :] = kv_buf[rel, s].astype(jnp.float32)
        keys = kv_wide[pl.ds(0, plane, stride=2), :].astype(jnp.bfloat16)
        vals = jnp.transpose(kv_wide[pl.ds(1, plane, stride=2), :]).astype(jnp.bfloat16)
        return keys, vals

    row_id = lax.broadcasted_iota(jnp.int32, (plane, 128), 0)
    lane_id = lax.broadcasted_iota(jnp.int32, (plane, 128), 1)
    slot_mine = lane_id == z * (NX * 2) + row_id // PAGE
    in_page = lax.rem(row_id[:, 0:1], PAGE).astype(jnp.float32)

    def bias_of(fill_row):
        fills = jnp.sum(jnp.where(slot_mine, fill_row, 0.0), axis=1, keepdims=True)
        return jnp.where(in_page < fills, 0.0, NEG)

    def attend(keys, vals, bias, q):
        top, total, grown = soften(mm(keys, q) * scale + bias)
        return top, total, mm(vals, grown)

    def absorb(d, k, streams, shared=None):
        keys, vals = shared or split_kv(nz - k if d == 0 else k)
        bias = bias_of(fill_buf[d, k - 1][0:1, :])
        for h in streams:
            top, total, acc = attend(keys, vals, bias, q_buf[d, k - 1, h])
            part_acc[d, k - 1, h] = acc
            part_ml[d, k - 1, h, 0:1, :] = top
            part_ml[d, k - 1, h, 1:2, :] = total

    def memory_block(b):
        here = pl.ds(pl.multiple_of(b * BLK, BLK), BLK)
        state = mem_m[...]
        kv = key_unit_t[b]
        errors = exact(state, kv[:, 0:BLK]) - kv[:, BLK:]
        grads = exact(errors, key_unit[b])
        read_t[b] = state
        push = momentum_ref[0, 0] * mem_s[...] - stride_ref[0, 0] * grads
        keep = retention_ref[0, 0] * jnp.where(halving_ref[0, b] == 1, 0.5, 1.0)
        mem_s[...] = push
        mem_m[...] = keep * state + push

    keys0, vals0 = split_kv(0)
    bias0 = bias_of(fill_own[0:1, :])
    for h in range(2):
        count = (h + 1) * half
        q = q_own[h]
        s_c = mm(keys0, q) * scale + bias0
        s_p = mm(persist_ref[0], q) * scale
        s_t = mm(keys_own[0:count, :], q) * scale
        order = lax.broadcasted_iota(jnp.int32, (count, half), 0)
        place = lax.broadcasted_iota(jnp.int32, (count, half), 1) + h * half
        s_t = jnp.where(order <= place, s_t, NEG)
        top_c, total_c, grown_c = soften(s_c)
        top_t, total_t, grown_t = soften(s_t)
        top_p, total_p, grown_p = soften(s_p)
        top = jnp.maximum(jnp.maximum(top_c, top_t), top_p)
        e_c, e_t, e_p = jnp.exp(top_c - top), jnp.exp(top_t - top), jnp.exp(top_p - top)
        persist_t = jnp.transpose(persist_ref[1].astype(jnp.float32)).astype(jnp.bfloat16)
        acc = mm(vals0, grown_c) * e_c + mm(values_t[:, 0:count], grown_t) * e_t
        home_acc[h] = acc + mm(persist_t, grown_p) * e_p
        home_ml[h, 0:1, :] = top
        home_ml[h, 1:2, :] = total_c * e_c + total_t * e_t + total_p * e_p

    def far(d):
        return d

    def gather_step(k, last):
        for d in range(2):
            f_done(d, k - 1).wait_recv()
            f_copy(d, k).start()
            for h in (d, 1 - d):
                q_done(d, h, k - 1).wait_recv()
                if h == far(d) or not last:
                    q_copy(d, h, k).start()

    def gather_loop(k, carry):
        gather_step(k, False)
        memory_block(k - 1)
        for d in range(2):
            absorb(d, k, (0, 1))
        return carry

    lax.fori_loop(1, depth - 1, gather_loop, 0)
    gather_step(depth - 1, True)
    spread_mid(wout)
    for d in range(2):
        absorb(d, depth - 1, (0, 1))

    def ring_copies(d, h, k):
        return (
            remote(
                send_acc.at[d, k, h],
                recv_acc.at[d, k, h],
                a_send.at[d, h, k],
                a_recv.at[d, h, k],
                ahead[1 - d],
            ),
            remote(
                send_ml.at[d, k, h],
                recv_ml.at[d, k, h],
                m_send.at[d, h, k],
                m_recv.at[d, h, k],
                ahead[1 - d],
            ),
        )

    def ring_send(d, h, k, acc, top, total):
        send_acc[d, k, h] = acc.astype(jnp.bfloat16)
        send_ml[d, k, h, 0:1, :] = top
        send_ml[d, k, h, 1:2, :] = total
        for c in ring_copies(d, h, k):
            c.start()

    def join(first, second):
        top = jnp.maximum(first[1], second[1])
        e_a, e_b = jnp.exp(first[1] - top), jnp.exp(second[1] - top)
        return first[0] * e_a + second[0] * e_b, top, first[2] * e_a + second[2] * e_b

    def received(d, h, k):
        for c in ring_copies(d, h, k):
            c.wait_recv()
        return (
            recv_acc[d, k, h].astype(jnp.float32),
            recv_ml[d, k, h, 0:1, :],
            recv_ml[d, k, h, 1:2, :],
        )

    def partial(d, h, k):
        return part_acc[d, k, h], part_ml[d, k, h, 0:1, :], part_ml[d, k, h, 1:2, :]

    def ring_join(d, h, k):
        ring_send(d, h, k, *join(partial(d, h, k), received(d, h, k + 1)))

    last = depth - 1
    opposite = split_kv(depth)
    for d in range(2):
        f_done(d, last).wait_recv()
        q_done(d, far(d), last).wait_recv()
        absorb(d, depth, (far(d),), opposite)
        ring_send(d, far(d), last, *partial(d, far(d), last))
    for d in range(2):
        ring_send(d, 1 - far(d), last - 1, *partial(d, 1 - far(d), last - 1))

    blocks = prefill // BLK

    def memory_rest(b, carry):
        memory_block(b)
        return carry

    lax.fori_loop(depth - 2, blocks, memory_rest, 0)
    new_state_ref[0] = mem_m[...]
    new_state_ref[1] = mem_s[...]
    spread_late(wout)

    def ring_loop(i, carry):
        for d in range(2):
            ring_join(d, far(d), last - i)
        for d in range(2):
            ring_join(d, 1 - far(d), last - 1 - i)
        return carry

    lax.fori_loop(1, last, ring_loop, 0)
    for d in range(2):
        ring_join(d, far(d), 0)

    for b in range(blocks):
        h, place = (b * BLK) // half, (b * BLK) % half
        cols = slice(place, place + BLK)
        gate_t[h, :, cols] = jax.nn.sigmoid(gate_t[h, :, cols]) * exact(
            read_t[b], query_unit_t[h, :, cols]
        )

    def head_copy(j):
        to_head = lax.rem(head + j, heads)
        return remote(
            hout_buf.at[to_head], hrecv.at[j], h_send.at[j], h_recv.at[j], (req, to_head)
        )

    for h in range(2):
        mine = home_acc[h], home_ml[h, 0:1, :], home_ml[h, 1:2, :]
        for d in (1 - h, h):
            mine = join(mine, received(d, h, 0))
        attended = mine[0] / mine[2]
        mean = jnp.mean(attended * attended, axis=0, keepdims=True)
        out = attended * lax.rsqrt(mean + UNIT_EPS) + gate_t[h]
        turned = jnp.transpose(out).astype(jnp.bfloat16)
        per = heads // 2
        for g in range(per):
            hout_buf[h * per + g] = turned[g * rows : (g + 1) * rows, :]

    for j in range(1, heads):
        head_copy(j).start()
    wout[0].wait_recv()
    for i in (4, 6, 7):
        wout[i].wait_recv()
    layer = mm(hout_buf[head], out_weight_ref[...]).astype(jnp.bfloat16).astype(jnp.float32)
    for j in range(1, heads):
        head_copy(j).wait_recv()
        group = lax.rem(head + heads - j, heads)
        layer = layer + mm(hrecv[j], wout_buf[group]).astype(jnp.bfloat16).astype(jnp.float32)
    layer_ref[...] = layer.astype(jnp.bfloat16)

    for c in tok + wout:
        c.wait_send()
    for j in range(1, heads):
        head_copy(j).wait_send()

    def kv_end(rel, carry):
        for j in range(1, NX):
            kv_copy(rel, j).wait_send()
        return carry

    lax.fori_loop(0, nz, kv_end, 0)

    def ring_end(d, h, k):
        q_done(d, h, k).wait_send()
        for c in ring_copies(d, h, k):
            c.wait_send()

    def ends(k, carry):
        for d in range(2):
            f_done(d, k).wait_send()
            for h in range(2):
                ring_end(d, h, k)
        return carry

    lax.fori_loop(0, last, ends, 0)
    for d in range(2):
        f_done(d, last).wait_send()
        ring_end(d, far(d), last)


def shards(
    tokens,
    gain,
    projection_weight,
    output_weight,
    persist,
    cache_page_slots,
    cached_length,
    page_keeper,
    page_slot_index,
    memory_state,
    retention,
    momentum,
    memory_step_scale,
    halving_updates,
    *,
    reqs,
    heads,
):
    nz, ny = reqs // NX, heads // CORES
    depth = nz // 2
    rows, width = tokens.shape[1], tokens.shape[2]
    prefill = rows * heads
    half = prefill // 2
    blocks = prefill // BLK
    span = cache_page_slots.shape[2] * 2
    bf, f32 = jnp.bfloat16, jnp.float32
    vmem = pl.BlockSpec(memory_space=pltpu.VMEM)
    smem = pl.BlockSpec(memory_space=pltpu.SMEM)
    hbm = pl.BlockSpec(memory_space=pl.ANY)
    sems = pltpu.SemaphoreType.DMA
    scratch = [
        pltpu.VMEM((heads, rows, width), bf),
        pltpu.VMEM((heads,) + output_weight.shape, bf),
        pltpu.VMEM((4 * width, HD), f32),
        pltpu.VMEM((4, width, HD), bf),
        pltpu.VMEM((prefill, width), bf),
        pltpu.VMEM((nz, NX, span, HD), bf),
        pltpu.VMEM((2, HD, half), bf),
        pltpu.VMEM((2, depth, 2, HD, half), bf),
        pltpu.VMEM((8, 128), f32),
        pltpu.VMEM((2, depth, 8, 128), f32),
        pltpu.VMEM((prefill, HD), bf),
        pltpu.VMEM((HD, prefill), bf),
        pltpu.VMEM((blocks, BLK, HD), f32),
        pltpu.VMEM((blocks, HD, 2 * BLK), f32),
        pltpu.VMEM((2, HD, half), f32),
        pltpu.VMEM((2, HD, half), f32),
        pltpu.VMEM((blocks, HD, HD), f32),
        pltpu.VMEM((HD, HD), f32),
        pltpu.VMEM((HD, HD), f32),
        pltpu.VMEM((NX * span, HD), f32),
        pltpu.VMEM((2, depth, 2, HD, half), f32),
        pltpu.VMEM((2, depth, 2, 2, half), f32),
        pltpu.VMEM((2, depth, 2, HD, half), bf),
        pltpu.VMEM((2, depth, 2, 2, half), f32),
        pltpu.VMEM((2, depth, 2, HD, half), bf),
        pltpu.VMEM((2, depth, 2, 2, half), f32),
        pltpu.VMEM((2, HD, half), f32),
        pltpu.VMEM((2, 2, half), f32),
        pltpu.VMEM((heads, rows, HD), bf),
        pltpu.VMEM((heads, rows, HD), bf),
        sems((8,)),
        sems((8,)),
        sems((8,)),
        sems((8,)),
        sems((nz, NX)),
        sems((nz, NX)),
        sems((nz,)),
        sems((2, 2, depth)),
        sems((2, 2, depth)),
        sems((2, depth)),
        sems((2, depth)),
        sems((2, 2, depth)),
        sems((2, 2, depth)),
        sems((2, 2, depth)),
        sems((2, 2, depth)),
        sems((heads,)),
        sems((heads,)),
    ]
    layer, state = pl.pallas_call(
        functools.partial(kernel, nz, ny),
        out_shape=(
            jax.ShapeDtypeStruct((rows, width), bf),
            jax.ShapeDtypeStruct((2, HD, HD), f32),
        ),
        in_specs=[vmem, vmem, vmem, vmem, vmem, hbm, smem, vmem, vmem, vmem, smem, smem, smem, smem],
        out_specs=(vmem, vmem),
        scratch_shapes=scratch,
        compiler_params=pltpu.CompilerParams(
            collective_id=0, has_side_effects=True, vmem_limit_bytes=56 * 1024 * 1024
        ),
    )(
        tokens.reshape(rows, width),
        gain.reshape(1, width),
        projection_weight.reshape(4 * width, HD),
        output_weight,
        persist,
        cache_page_slots.reshape(cache_page_slots.shape[1], span, HD),
        cached_length,
        page_keeper,
        page_slot_index,
        memory_state.reshape(2, HD, HD),
        retention,
        momentum,
        memory_step_scale,
        halving_updates,
    )
    return layer.reshape(tokens.shape), state.reshape(memory_state.shape)


def solution(mesh):
    in_specs = (
        P("req", "head", None),
        P(),
        P(None, None, "head"),
        P("head", None),
        P(None, None, "head"),
        P("req", None, None, None, "head"),
        P("req"),
        P("req", None),
        P("req", None),
        P(None, "req", "head", None, None),
        P("req", "head"),
        P("req", "head"),
        P("req", "head"),
        P("req", None),
    )
    out_specs = (P("req", "head", None), P(None, "req", "head", None, None))
    body = functools.partial(shards, reqs=mesh.shape["req"], heads=mesh.shape["head"])
    return jax.shard_map(body, mesh=mesh, in_specs=in_specs, out_specs=out_specs, check_vma=False)
```

```python
import functools
import math

import jax
import jax.numpy as jnp
from jax import lax
from jax.experimental import pallas as pl
from jax.experimental.pallas import tpu as pltpu
from jax.sharding import PartitionSpec as P

HD = 128
BLK = 64
PAGE = 32
NX = 4
CORES = 2
REACH = 5
MESH = pl.DeviceIdType.MESH
NEG = -1e30
FLOOR = -5e29
NORM_EPS = 1e-05
UNIT_EPS = 1e-06
HIGHEST = lax.Precision.HIGHEST


def mm(left, right):
    return jnp.dot(left, right, preferred_element_type=jnp.float32)


def exact(left, right):
    return jnp.dot(left, right, precision=HIGHEST, preferred_element_type=jnp.float32)


def soften(scores):
    top = jnp.maximum(jnp.max(scores, axis=0, keepdims=True), FLOOR)
    grown = jnp.exp(scores - top)
    return top, jnp.sum(grown, axis=0, keepdims=True), grown.astype(jnp.bfloat16)


def kernel(
    nz,
    ny,
    tokens_ref,
    gain_ref,
    weight_ref,
    out_weight_ref,
    persist_ref,
    cache_ref,
    length_ref,
    keeper_ref,
    slot_ref,
    state_ref,
    retention_ref,
    momentum_ref,
    stride_ref,
    halving_ref,
    layer_ref,
    new_state_ref,
    tok_buf,
    wout_buf,
    wide,
    w_parts,
    normed,
    kv_home,
    kv_buf,
    q_own,
    q_buf,
    fill_own,
    fill_buf,
    keys_own,
    values_t,
    key_unit,
    key_unit_t,
    value_f,
    query_unit_t,
    gate_t,
    extra_t,
    mem_m,
    mem_s,
    kv_wide,
    keys_far,
    values_far,
    part_acc,
    part_ml,
    send_acc,
    send_ml,
    recv_acc,
    recv_ml,
    home_acc,
    home_ml,
    hout_buf,
    hrecv,
    tok_send,
    tok_recv,
    wo_send,
    wo_recv,
    h0_send,
    h0_recv,
    h0_local,
    kv_send,
    kv_recv,
    kv_local,
    q_send,
    q_recv,
    f_send,
    f_recv,
    a_send,
    a_recv,
    m_send,
    m_recv,
    h_send,
    h_recv,
):
    req = lax.axis_index("req")
    head = lax.axis_index("head")
    z, x = req // NX, lax.rem(req, NX)
    y, core = head // CORES, lax.rem(head, CORES)
    heads = ny * CORES
    rows = tokens_ref.shape[0]
    prefill = heads * rows
    half = prefill // 2
    width = tokens_ref.shape[1]
    span = cache_ref.shape[1]
    plane = NX * span // 2
    depth = nz // 2
    reach = min(REACH, depth - 1)
    beyond = depth - reach
    scale = 1.0 / math.sqrt(HD)

    partner = y * CORES + (1 - core)
    right_head = lax.rem(y + 1, ny) * CORES + core
    left_head = lax.rem(y + ny - 1, ny) * CORES + core
    anti_head = lax.rem(y + 2, ny) * CORES + core
    z_next = (lax.rem(z + 1, nz) * NX + x, head)
    z_back = (lax.rem(z + nz - 1, nz) * NX + x, head)
    ahead = (z_next, z_back)

    barrier = pltpu.get_barrier_semaphore()
    for hop in range(-beyond, beyond + 1):
        for j in range(NX):
            if hop or j:
                peer = (lax.rem(z + nz + hop, nz) * NX + lax.rem(x + j, NX), head)
                pl.semaphore_signal(barrier, inc=1, device_id=peer, device_id_type=MESH)
    for j in range(1, heads):
        peer = (req, lax.rem(head + j, heads))
        pl.semaphore_signal(barrier, inc=1, device_id=peer, device_id_type=MESH)
    pl.semaphore_wait(barrier, (2 * beyond + 1) * NX - 1 + heads - 1)

    def remote(src, dst, send, recv, device):
        return pltpu.make_async_remote_copy(
            src_ref=src,
            dst_ref=dst,
            send_sem=send,
            recv_sem=recv,
            device_id=device,
            device_id_type=MESH,
        )

    def spread(own, buf, send, recv):
        cut = own.shape[0] // 2
        low, high = pl.ds(0, cut), pl.ds(cut, cut)
        to = lambda src, dst, i, g: remote(src, dst, send.at[i], recv.at[i], (req, g))
        from_left = buf.at[left_head]
        from_right = buf.at[right_head]
        mine = buf.at[head]
        return (
            to(own, mine, 0, partner),
            to(own.at[low], buf.at[head, low], 1, right_head),
            to(own.at[high], buf.at[head, high], 2, right_head),
            to(own.at[low], buf.at[head, low], 3, left_head),
            to(own.at[high], buf.at[head, high], 4, left_head),
            to(buf.at[left_head, low], buf.at[left_head, low], 5, right_head),
            to(buf.at[right_head, high], buf.at[right_head, high], 6, left_head),
            to(from_left, from_left, 7, partner),
            to(from_right, from_right, 8, partner),
            to(buf.at[anti_head, low], buf.at[anti_head, low], 9, partner),
            to(buf.at[anti_head, high], buf.at[anti_head, high], 10, partner),
        )

    def spread_begin(c):
        for i in (1, 4, 0, 2, 3):
            c[i].start()

    def spread_mid(c):
        for first, then in ((1, 5), (4, 6), (2, 7), (3, 8)):
            c[first].wait_recv()
            c[then].start()

    def spread_late(c):
        for first, then in ((5, 9), (6, 10)):
            c[first].wait_recv()
            c[then].start()

    tok = spread(tokens_ref, tok_buf, tok_send, tok_recv)
    wout = spread(out_weight_ref, wout_buf, wo_send, wo_recv)
    spread_begin(tok)

    def home_copy(j):
        to_x = lax.rem(x + j, NX)
        return remote(
            cache_ref.at[z * NX + to_x],
            kv_home.at[x],
            h0_send.at[j],
            h0_recv.at[j],
            (z * NX + to_x, head),
        )

    def home_stay():
        return pltpu.make_async_copy(cache_ref.at[req], kv_home.at[x], h0_local)

    def kv_copy(d, k, j):
        sign = 1 - 2 * d
        to_x = lax.rem(x + j, NX)
        asker = lax.rem(z + nz - sign * k, nz)
        over = max(k - reach, 0) if isinstance(k, int) else 0
        server = lax.rem(z + nz - sign * over, nz)
        return remote(
            cache_ref.at[asker * NX + to_x],
            kv_buf.at[d, k - 1, x],
            kv_send.at[d, k - 1, j],
            kv_recv.at[d, k - 1, j],
            (server * NX + to_x, head),
        )

    def kv_stay(d, k):
        asker = lax.rem(z + nz - (1 - 2 * d) * k, nz)
        return pltpu.make_async_copy(
            cache_ref.at[asker * NX + x], kv_buf.at[d, k - 1, x], kv_local.at[d, k - 1]
        )

    side = x // (NX // 2)
    for j in range(NX):
        kv_copy(side, depth, j).start()
    for k in range(depth - 1, reach, -1):
        for d in range(2):
            for j in range(NX):
                kv_copy(d, k, j).start()

    wide[...] = weight_ref[...].astype(jnp.float32)
    for part in range(4):
        w_parts[part] = wide[pl.ds(part, width, stride=4), :].astype(jnp.bfloat16)

    spread_mid(tok)
    for k in range(1, reach + 1):
        for d in range(2):
            kv_stay(d, k).start()
            for j in range(1, NX):
                kv_copy(d, k, j).start()
    home_stay().start()
    for j in range(1, NX):
        home_copy(j).start()

    ids = lax.broadcasted_iota(jnp.int32, (1, 128), 1)
    filled = jnp.clip(length_ref[0] - ids * PAGE, 0, PAGE).astype(jnp.float32)
    slot_of = keeper_ref[...] * 2 + slot_ref[...]
    filled_t = jnp.transpose(jnp.broadcast_to(filled, (128, 128)))
    slot_t = jnp.transpose(jnp.broadcast_to(slot_of.astype(jnp.float32), (128, 128)))
    lanes_f = lax.broadcasted_iota(jnp.int32, (128, 128), 1).astype(jnp.float32)
    slot_fill = jnp.sum(jnp.where(slot_t == lanes_f, filled_t, 0.0), axis=0, keepdims=True)
    fill_own[...] = jnp.broadcast_to(slot_fill, (8, 128))

    gain_f = gain_ref[...].astype(jnp.float32)
    gain_row = jnp.concatenate([gain_f[i : i + 1, :] for i in range(width // 128)], axis=1)

    def norm_block(block, g):
        x_f = block.astype(jnp.float32)
        mean = jnp.mean(x_f * x_f, axis=-1, keepdims=True)
        scaled = x_f * lax.rsqrt(mean + NORM_EPS) * gain_row
        normed[pl.ds(pl.multiple_of(g * rows, rows), rows), :] = scaled.astype(jnp.bfloat16)

    norm_block(tokens_ref[...], head)
    norm_block(tok_buf[left_head], left_head)
    norm_block(tok_buf[right_head], right_head)
    spread_late(tok)
    spread_begin(wout)
    norm_block(tok_buf[anti_head], anti_head)
    tok[0].wait_recv()
    norm_block(tok_buf[partner], partner)
    flip = lambda g: (g // CORES) * CORES + (1 - core)
    for i, g in ((7, left_head), (8, right_head)):
        tok[i].wait_recv()
        norm_block(tok_buf[flip(g)], flip(g))
    tok[9].wait_recv()
    tok[10].wait_recv()
    norm_block(tok_buf[flip(anti_head)], flip(anti_head))

    q_t = jnp.transpose(mm(normed[...], w_parts[0]))
    for h in range(2):
        q_own[h] = q_t[:, h * half : (h + 1) * half].astype(jnp.bfloat16)

    def q_copy(d, h, k):
        src = q_own.at[h] if isinstance(k, int) and k == 0 else q_buf.at[d, k - 1, h]
        return remote(
            src, q_buf.at[d, k, h], q_send.at[d, h, k], q_recv.at[d, h, k], ahead[d]
        )

    def q_done(d, h, k):
        place = q_buf.at[d, k, h]
        return remote(place, place, q_send.at[d, h, k], q_recv.at[d, h, k], ahead[d])

    def f_done(d, k):
        place = fill_buf.at[d, k]
        return remote(place, place, f_send.at[d, k], f_recv.at[d, k], ahead[d])

    def f_copy(d, k):
        src = fill_own if isinstance(k, int) and k == 0 else fill_buf.at[d, k - 1]
        return remote(src, fill_buf.at[d, k], f_send.at[d, k], f_recv.at[d, k], ahead[d])

    for d in range(2):
        f_copy(d, 0).start()
        for h in (d, 1 - d):
            q_copy(d, h, 0).start()

    def unit_columns(v):
        return v * lax.rsqrt(jnp.sum(v * v, axis=0, keepdims=True) + UNIT_EPS)

    k_bf = mm(normed[...], w_parts[1]).astype(jnp.bfloat16)
    keys_own[...] = k_bf
    k_f = k_bf.astype(jnp.float32)
    k_unit = k_f * lax.rsqrt(jnp.sum(k_f * k_f, axis=-1, keepdims=True) + UNIT_EPS)
    v_bf = mm(normed[...], w_parts[2]).astype(jnp.bfloat16)
    v_t = jnp.transpose(v_bf.astype(jnp.float32))
    k_unit_t = jnp.transpose(k_unit)
    gates = jnp.transpose(mm(normed[...], w_parts[3]))
    values_t[...] = v_t.astype(jnp.bfloat16)
    units = unit_columns(jnp.concatenate([q_own[0], q_own[1]], axis=1).astype(jnp.float32))
    for b in range(prefill // BLK):
        key_unit[b] = k_unit[b * BLK : (b + 1) * BLK, :]
    for p in range(prefill // (2 * BLK)):
        columns = slice(p * 2 * BLK, (p + 1) * 2 * BLK)
        key_unit_t[p] = k_unit_t[:, columns]
        value_f[p] = v_t[:, columns]
        query_unit_t[p] = units[:, columns]
        gate_t[p] = gates[:, columns]
    mem_m[...] = state_ref[0]
    mem_s[...] = state_ref[1]

    def pick(blocks):
        count = len(blocks) * span
        for s, block in enumerate(blocks):
            kv_wide[s * span : (s + 1) * span, :] = block.astype(jnp.float32)
        keys = kv_wide[pl.ds(0, count // 2, stride=2), :].astype(jnp.bfloat16)
        vals = jnp.transpose(kv_wide[pl.ds(1, count // 2, stride=2), :]).astype(jnp.bfloat16)
        return keys, vals

    def split_near(d, k):
        kv_stay(d, k).wait()
        for j in range(1, NX):
            kv_copy(d, k, j).wait_recv()
        return pick([kv_buf[d, k - 1, s] for s in range(NX)])

    far_sides = tuple(tuple(range(d * NX // 2, (d + 1) * NX // 2)) for d in range(2))
    far_rows = (beyond + 1) * plane - plane // 2

    def split_far(d):
        for k in range(reach, depth + 1):
            if k == reach:
                keys, vals = split_near(d, k)
            elif k < depth:
                for j in range(NX):
                    kv_copy(d, k, j).wait_recv()
                keys, vals = pick([kv_buf[d, k - 1, s] for s in range(NX)])
            else:
                for s in far_sides[d]:
                    kv_copy(d, k, lax.rem(x + NX - s, NX)).wait_recv()
                keys, vals = pick([kv_buf[d, k - 1, s] for s in far_sides[d]])
            at = (k - reach) * plane
            keys_far[d, at : at + keys.shape[0], :] = keys
            values_far[d, :, at : at + keys.shape[0]] = vals

    def bias_of(fill_row, server, first, count):
        row_id = lax.broadcasted_iota(jnp.int32, (count, 128), 0)
        lane_id = lax.broadcasted_iota(jnp.int32, (count, 128), 1)
        slot_mine = lane_id == server * (NX * 2) + first + row_id // PAGE
        fills = jnp.sum(jnp.where(slot_mine, fill_row, 0.0), axis=1, keepdims=True)
        in_page = lax.rem(row_id[:, 0:1], PAGE).astype(jnp.float32)
        return jnp.where(in_page < fills, 0.0, NEG)

    def attend(keys, vals, bias, q):
        top, total, grown = soften(mm(keys, q) * scale + bias)
        return top, total, mm(vals, grown)

    def keep_part(d, k, h, result):
        top, total, acc = result
        part_acc[d, k - 1, h] = acc
        part_ml[d, k - 1, h, 0:1, :] = top
        part_ml[d, k - 1, h, 1:2, :] = total

    def absorb(d, k):
        keys, vals = split_near(d, k)
        bias = bias_of(fill_buf[d, k - 1][0:1, :], z, 0, plane)
        for h in range(2):
            keep_part(d, k, h, attend(keys, vals, bias, q_buf[d, k - 1, h]))

    def memory_pair(p):
        reads = []
        for u in range(2):
            columns = slice(u * BLK, (u + 1) * BLK)
            b = 2 * p + u
            state = mem_m[...]
            reads.append(exact(state, query_unit_t[p][:, columns]))
            errors = exact(state, key_unit_t[p][:, columns]) - value_f[p][:, columns]
            grads = exact(errors, key_unit[b])
            push = momentum_ref[0, 0] * mem_s[...] - stride_ref[0, 0] * grads
            keep = retention_ref[0, 0] * jnp.where(halving_ref[0, b] == 1, 0.5, 1.0)
            mem_s[...] = push
            mem_m[...] = keep * state + push
        extra_t[p] = jax.nn.sigmoid(gate_t[p]) * jnp.concatenate(reads, axis=1)

    def own_attention():
        home_stay().wait()
        for j in range(1, NX):
            home_copy(j).wait_recv()
        keys0, vals0 = pick([kv_home[s] for s in range(NX)])
        bias0 = bias_of(fill_own[0:1, :], z, 0, plane)
        persist_t = jnp.transpose(persist_ref[1].astype(jnp.float32)).astype(jnp.bfloat16)
        for h in range(2):
            count = (h + 1) * half
            q = q_own[h]
            s_c = mm(keys0, q) * scale + bias0
            s_p = mm(persist_ref[0], q) * scale
            s_t = mm(keys_own[0:count, :], q) * scale
            order = lax.broadcasted_iota(jnp.int32, (count, half), 0)
            place = lax.broadcasted_iota(jnp.int32, (count, half), 1) + h * half
            s_t = jnp.where(order <= place, s_t, NEG)
            top_c, total_c, grown_c = soften(s_c)
            top_t, total_t, grown_t = soften(s_t)
            top_p, total_p, grown_p = soften(s_p)
            top = jnp.maximum(jnp.maximum(top_c, top_t), top_p)
            e_c, e_t, e_p = jnp.exp(top_c - top), jnp.exp(top_t - top), jnp.exp(top_p - top)
            acc = mm(vals0, grown_c) * e_c + mm(values_t[:, 0:count], grown_t) * e_t
            home_acc[h] = acc + mm(persist_t, grown_p) * e_p
            home_ml[h, 0:1, :] = top
            home_ml[h, 1:2, :] = total_c * e_c + total_t * e_t + total_p * e_p

    order_of = lambda d: (d, 1 - d)

    def gather_step(k):
        for d in range(2):
            f_done(d, k - 1).wait_recv()
            f_copy(d, k).start()
            for h in order_of(d):
                q_done(d, h, k - 1).wait_recv()
                q_copy(d, h, k).start()

    for d in range(2):
        split_far(d)

    def gather_loop(k, carry):
        gather_step(k)
        for d in range(2):
            absorb(d, k)
        return carry

    lax.fori_loop(1, reach, gather_loop, 0)
    spread_mid(wout)

    def ring_copies(d, h, k):
        return (
            remote(
                send_acc.at[d, k, h],
                recv_acc.at[d, k, h],
                a_send.at[d, h, k],
                a_recv.at[d, h, k],
                ahead[1 - d],
            ),
            remote(
                send_ml.at[d, k, h],
                recv_ml.at[d, k, h],
                m_send.at[d, h, k],
                m_recv.at[d, h, k],
                ahead[1 - d],
            ),
        )

    def ring_send(d, h, k, acc, top, total):
        send_acc[d, k, h] = acc.astype(jnp.bfloat16)
        send_ml[d, k, h, 0:1, :] = top
        send_ml[d, k, h, 1:2, :] = total
        for c in ring_copies(d, h, k):
            c.start()

    def join(first, second):
        top = jnp.maximum(first[1], second[1])
        e_a, e_b = jnp.exp(first[1] - top), jnp.exp(second[1] - top)
        return first[0] * e_a + second[0] * e_b, top, first[2] * e_a + second[2] * e_b

    def received(d, h, k):
        for c in ring_copies(d, h, k):
            c.wait_recv()
        return (
            recv_acc[d, k, h].astype(jnp.float32),
            recv_ml[d, k, h, 0:1, :],
            recv_ml[d, k, h, 1:2, :],
        )

    def partial(d, h, k):
        return part_acc[d, k, h], part_ml[d, k, h, 0:1, :], part_ml[d, k, h, 1:2, :]

    def ring_join(d, h, k):
        ring_send(d, h, k, *join(partial(d, h, k), received(d, h, k + 1)))

    last = reach - 1
    biases = []
    for d in range(2):
        f_done(d, last).wait_recv()
        fill_row = fill_buf[d, last][0:1, :]
        pieces = []
        for hop in range(beyond + 1):
            server = lax.rem(z + nz + (1 - 2 * d) * hop, nz)
            first, count = (d * NX, plane // 2) if hop == beyond else (0, plane)
            pieces.append(bias_of(fill_row, server, first, count))
        biases.append(jnp.concatenate(pieces, axis=0))
    for i in range(2):
        for d in range(2):
            h = order_of(d)[i]
            q_done(d, h, last).wait_recv()
            top, total, acc = attend(
                keys_far[d], values_far[d], biases[d], q_buf[d, last, h]
            )
            ring_send(d, h, last, acc, top, total)

    own_attention()
    spread_late(wout)
    pairs = prefill // (2 * BLK)

    def ring_loop(i, carry):
        for n in range(2):
            for d in range(2):
                ring_join(d, order_of(d)[n], last - i)
        pl.when(i <= pairs)(lambda: memory_pair(i - 1))
        return carry

    lax.fori_loop(1, reach, ring_loop, 0)
    for p in range(reach - 1, pairs):
        memory_pair(p)
    new_state_ref[0] = mem_m[...]
    new_state_ref[1] = mem_s[...]

    def head_copy(g):
        return remote(hout_buf.at[g], hrecv.at[head], h_send.at[g], h_recv.at[head], (req, g))

    def head_arrival(g):
        return remote(hout_buf.at[g], hrecv.at[g], h_send.at[g], h_recv.at[g], (req, g))

    per = heads // 2
    for h in range(2):
        mine = home_acc[h], home_ml[h, 0:1, :], home_ml[h, 1:2, :]
        for d in (h, 1 - h):
            mine = join(mine, received(d, h, 0))
        attended = mine[0] / mine[2]
        mean = jnp.mean(attended * attended, axis=0, keepdims=True)
        some = pairs // 2
        extra = jnp.concatenate([extra_t[h * some + p] for p in range(some)], axis=1)
        out = attended * lax.rsqrt(mean + UNIT_EPS) + extra
        turned = jnp.transpose(out).astype(jnp.bfloat16)
        for g in range(h * per, (h + 1) * per):
            hout_buf[g] = turned[(g - h * per) * rows : (g - h * per + 1) * rows, :]
        for g in range(h * per, (h + 1) * per):
            pl.when(g != head)(lambda g=g: head_copy(g).start())

    for i in (0, 7, 8, 9, 10):
        wout[i].wait_recv()
    layer = mm(hout_buf[head], out_weight_ref[...]).astype(jnp.bfloat16).astype(jnp.float32)
    for j in range(1, heads):
        group = lax.rem(head + j, heads)
        head_arrival(group).wait_recv()
        layer = layer + mm(hrecv[group], wout_buf[group]).astype(jnp.bfloat16).astype(jnp.float32)
    layer_ref[...] = layer.astype(jnp.bfloat16)

    for c in tok + wout:
        c.wait_send()
    for j in range(1, heads):
        head_copy(lax.rem(head + j, heads)).wait_send()
    for j in range(1, NX):
        home_copy(j).wait_send()
        for k in range(1, reach + 1):
            for d in range(2):
                kv_copy(d, k, j).wait_send()
    for j in range(NX):
        for k in range(reach + 1, depth):
            for d in range(2):
                kv_copy(d, k, j).wait_send()
        kv_copy(side, depth, j).wait_send()

    def ends(k, carry):
        for d in range(2):
            f_done(d, k).wait_send()
            for h in range(2):
                q_done(d, h, k).wait_send()
                for c in ring_copies(d, h, k):
                    c.wait_send()
        return carry

    lax.fori_loop(0, reach, ends, 0)


def settle(layer_ref, state_ref, layer_out, state_out):
    layer_out[...] = layer_ref[...]
    state_out[...] = state_ref[...]


def shards(
    tokens,
    gain,
    projection_weight,
    output_weight,
    persist,
    cache_page_slots,
    cached_length,
    page_keeper,
    page_slot_index,
    memory_state,
    retention,
    momentum,
    memory_step_scale,
    halving_updates,
    *,
    reqs,
    heads,
):
    nz, ny = reqs // NX, heads // CORES
    depth = nz // 2
    rows, width = tokens.shape[1], tokens.shape[2]
    prefill = rows * heads
    half = prefill // 2
    blocks = prefill // BLK
    span = cache_page_slots.shape[2] * 2
    bf, f32 = jnp.bfloat16, jnp.float32
    vmem = pl.BlockSpec(memory_space=pltpu.VMEM)
    smem = pl.BlockSpec(memory_space=pltpu.SMEM)
    hbm = pl.BlockSpec(memory_space=pl.ANY)
    sems = pltpu.SemaphoreType.DMA
    reach = min(REACH, depth - 1)
    pairs = blocks // 2
    rings = (2, reach, 2)
    far_rows = (depth - reach + 1) * NX * span // 2 - NX * span // 4
    scratch = [
        pltpu.VMEM((heads, rows, width), bf),
        pltpu.VMEM((heads,) + output_weight.shape, bf),
        pltpu.VMEM((4 * width, HD), f32),
        pltpu.VMEM((4, width, HD), bf),
        pltpu.VMEM((prefill, width), bf),
        pltpu.VMEM((NX, span, HD), bf),
        pltpu.VMEM((2, depth, NX, span, HD), bf),
        pltpu.VMEM((2, HD, half), bf),
        pltpu.VMEM(rings + (HD, half), bf),
        pltpu.VMEM((8, 128), f32),
        pltpu.VMEM((2, reach, 8, 128), f32),
        pltpu.VMEM((prefill, HD), bf),
        pltpu.VMEM((HD, prefill), bf),
        pltpu.VMEM((blocks, BLK, HD), f32),
        pltpu.VMEM((pairs, HD, 2 * BLK), f32),
        pltpu.VMEM((pairs, HD, 2 * BLK), f32),
        pltpu.VMEM((pairs, HD, 2 * BLK), f32),
        pltpu.VMEM((pairs, HD, 2 * BLK), f32),
        pltpu.VMEM((pairs, HD, 2 * BLK), f32),
        pltpu.VMEM((HD, HD), f32),
        pltpu.VMEM((HD, HD), f32),
        pltpu.VMEM((NX * span, HD), f32),
        pltpu.VMEM((2, far_rows, HD), bf),
        pltpu.VMEM((2, HD, far_rows), bf),
        pltpu.VMEM(rings + (HD, half), f32),
        pltpu.VMEM(rings + (2, half), f32),
        pltpu.VMEM(rings + (HD, half), bf),
        pltpu.VMEM(rings + (2, half), f32),
        pltpu.VMEM(rings + (HD, half), bf),
        pltpu.VMEM(rings + (2, half), f32),
        pltpu.VMEM((2, HD, half), f32),
        pltpu.VMEM((2, 2, half), f32),
        pltpu.VMEM((heads, rows, HD), bf),
        pltpu.VMEM((heads, rows, HD), bf),
        sems((11,)),
        sems((11,)),
        sems((11,)),
        sems((11,)),
        sems((NX,)),
        sems((NX,)),
        sems,
        sems((2, depth, NX)),
        sems((2, depth, NX)),
        sems((2, depth)),
        sems((2, 2, reach)),
        sems((2, 2, reach)),
        sems((2, reach)),
        sems((2, reach)),
        sems((2, 2, reach)),
        sems((2, 2, reach)),
        sems((2, 2, reach)),
        sems((2, 2, reach)),
        sems((heads,)),
        sems((heads,)),
    ]
    layer, state = pl.pallas_call(
        functools.partial(kernel, nz, ny),
        out_shape=(
            jax.ShapeDtypeStruct((rows, width), bf),
            jax.ShapeDtypeStruct((2, HD, HD), f32),
        ),
        in_specs=[vmem] * 5 + [hbm, smem, vmem, vmem, vmem] + [smem] * 4,
        out_specs=(vmem, vmem),
        scratch_shapes=scratch,
        compiler_params=pltpu.CompilerParams(
            collective_id=0, has_side_effects=True, vmem_limit_bytes=56 * 1024 * 1024
        ),
    )(
        tokens.reshape(rows, width),
        gain.reshape(width // 128, 128),
        projection_weight.reshape(4 * width, HD),
        output_weight,
        persist,
        cache_page_slots.reshape(cache_page_slots.shape[1], span, HD),
        cached_length,
        page_keeper,
        page_slot_index,
        memory_state.reshape(2, HD, HD),
        retention,
        momentum,
        memory_step_scale,
        halving_updates,
    )
    layer, state = pl.pallas_call(
        settle,
        out_shape=(
            jax.ShapeDtypeStruct((rows, width), bf),
            jax.ShapeDtypeStruct((2, HD, HD), f32),
        ),
        in_specs=[vmem, vmem],
        out_specs=(vmem, vmem),
    )(layer, state)
    return layer.reshape(tokens.shape), state.reshape(memory_state.shape)


def solution(mesh):
    in_specs = (
        P("req", "head", None),
        P(),
        P(None, None, "head"),
        P("head", None),
        P(None, None, "head"),
        P("req", None, None, None, "head"),
        P("req"),
        P("req", None),
        P("req", None),
        P(None, "req", "head", None, None),
        P("req", "head"),
        P("req", "head"),
        P("req", "head"),
        P("req", None),
    )
    out_specs = (P("req", "head", None), P(None, "req", "head", None, None))
    body = functools.partial(shards, reqs=mesh.shape["req"], heads=mesh.shape["head"])
    return jax.shard_map(body, mesh=mesh, in_specs=in_specs, out_specs=out_specs, check_vma=False)
```

```python
import functools
import math

import jax
import jax.numpy as jnp
from jax import lax
from jax.experimental import pallas as pl
from jax.experimental.pallas import tpu as pltpu
from jax.sharding import PartitionSpec as P

HD = 128
BLK = 64
PAGE = 32
NX = 4
CORES = 2
REACH = 5
CHUNK = 128
MESH = pl.DeviceIdType.MESH
NEG = -1e30
FLOOR = -5e29
NORM_EPS = 1e-05
UNIT_EPS = 1e-06
HIGHEST = lax.Precision.HIGHEST


def mm(left, right):
    return jnp.dot(left, right, preferred_element_type=jnp.float32)


def exact(left, right):
    return jnp.dot(left, right, precision=HIGHEST, preferred_element_type=jnp.float32)


def soften(scores):
    top = jnp.maximum(jnp.max(scores, axis=0, keepdims=True), FLOOR)
    grown = jnp.exp(scores - top)
    return top, jnp.sum(grown, axis=0, keepdims=True), grown.astype(jnp.bfloat16)


def kernel(
    nz,
    ny,
    tokens_ref,
    gain_ref,
    weight_ref,
    out_weight_ref,
    persist_ref,
    cache_ref,
    length_ref,
    keeper_ref,
    slot_ref,
    state_ref,
    retention_ref,
    momentum_ref,
    stride_ref,
    halving_ref,
    layer_ref,
    new_state_ref,
    tok_buf,
    wout_buf,
    wide,
    w_parts,
    normed,
    kv_home,
    kv_buf,
    q_own,
    q_buf,
    fill_own,
    fill_buf,
    keys_own,
    values_t,
    key_unit,
    key_unit_t,
    value_f,
    query_unit_t,
    gate_t,
    extra_t,
    mem_m,
    mem_s,
    kv_wide,
    keys_far,
    values_far,
    part_acc,
    part_ml,
    send_acc,
    send_ml,
    recv_acc,
    recv_ml,
    home_acc,
    home_ml,
    hout_buf,
    hrecv,
    tok_send,
    tok_recv,
    wo_send,
    wo_recv,
    h0_send,
    h0_recv,
    h0_local,
    kv_send,
    kv_recv,
    kv_local,
    q_send,
    q_recv,
    f_send,
    f_recv,
    a_send,
    a_recv,
    m_send,
    m_recv,
    h_send,
    h_recv,
):
    req = lax.axis_index("req")
    head = lax.axis_index("head")
    z, x = req // NX, lax.rem(req, NX)
    y, core = head // CORES, lax.rem(head, CORES)
    heads = ny * CORES
    rows = tokens_ref.shape[0]
    prefill = heads * rows
    chunks = prefill // CHUNK
    width = tokens_ref.shape[1]
    span = cache_ref.shape[1]
    plane = NX * span // 2
    depth = nz // 2
    reach = min(REACH, depth - 1)
    beyond = depth - reach
    scale = 1.0 / math.sqrt(HD)

    partner = y * CORES + (1 - core)
    right_head = lax.rem(y + 1, ny) * CORES + core
    left_head = lax.rem(y + ny - 1, ny) * CORES + core
    anti_head = lax.rem(y + 2, ny) * CORES + core
    z_next = (lax.rem(z + 1, nz) * NX + x, head)
    z_back = (lax.rem(z + nz - 1, nz) * NX + x, head)
    ahead = (z_next, z_back)

    barrier = pltpu.get_barrier_semaphore()
    for hop in range(-beyond, beyond + 1):
        for j in range(NX):
            if hop or j:
                peer = (lax.rem(z + nz + hop, nz) * NX + lax.rem(x + j, NX), head)
                pl.semaphore_signal(barrier, inc=1, device_id=peer, device_id_type=MESH)
    for j in range(1, heads):
        peer = (req, lax.rem(head + j, heads))
        pl.semaphore_signal(barrier, inc=1, device_id=peer, device_id_type=MESH)
    pl.semaphore_wait(barrier, (2 * beyond + 1) * NX - 1 + heads - 1)

    def remote(src, dst, send, recv, device):
        return pltpu.make_async_remote_copy(
            src_ref=src,
            dst_ref=dst,
            send_sem=send,
            recv_sem=recv,
            device_id=device,
            device_id_type=MESH,
        )

    def spread(own, buf, send, recv):
        cut = own.shape[0] // 2
        low, high = pl.ds(0, cut), pl.ds(cut, cut)
        to = lambda src, dst, i, g: remote(src, dst, send.at[i], recv.at[i], (req, g))
        from_left = buf.at[left_head]
        from_right = buf.at[right_head]
        mine = buf.at[head]
        return (
            to(own, mine, 0, partner),
            to(own.at[low], buf.at[head, low], 1, right_head),
            to(own.at[high], buf.at[head, high], 2, right_head),
            to(own.at[low], buf.at[head, low], 3, left_head),
            to(own.at[high], buf.at[head, high], 4, left_head),
            to(buf.at[left_head, low], buf.at[left_head, low], 5, right_head),
            to(buf.at[right_head, high], buf.at[right_head, high], 6, left_head),
            to(from_left, from_left, 7, partner),
            to(from_right, from_right, 8, partner),
            to(buf.at[anti_head, low], buf.at[anti_head, low], 9, partner),
            to(buf.at[anti_head, high], buf.at[anti_head, high], 10, partner),
        )

    def spread_begin(c):
        for i in (1, 4, 0, 2, 3):
            c[i].start()

    def spread_mid(c):
        for first, then in ((1, 5), (4, 6), (2, 7), (3, 8)):
            c[first].wait_recv()
            c[then].start()

    def spread_late(c):
        for first, then in ((5, 9), (6, 10)):
            c[first].wait_recv()
            c[then].start()

    tok = spread(tokens_ref, tok_buf, tok_send, tok_recv)
    wout = spread(out_weight_ref, wout_buf, wo_send, wo_recv)
    spread_begin(tok)

    def home_copy(j):
        to_x = lax.rem(x + j, NX)
        return remote(
            cache_ref.at[z * NX + to_x],
            kv_home.at[x],
            h0_send.at[j],
            h0_recv.at[j],
            (z * NX + to_x, head),
        )

    def home_stay():
        return pltpu.make_async_copy(cache_ref.at[req], kv_home.at[x], h0_local)

    def kv_copy(d, k, j):
        sign = 1 - 2 * d
        to_x = lax.rem(x + j, NX)
        asker = lax.rem(z + nz - sign * k, nz)
        over = max(k - reach, 0) if isinstance(k, int) else 0
        server = lax.rem(z + nz - sign * over, nz)
        return remote(
            cache_ref.at[asker * NX + to_x],
            kv_buf.at[d, k - 1, x],
            kv_send.at[d, k - 1, j],
            kv_recv.at[d, k - 1, j],
            (server * NX + to_x, head),
        )

    def kv_stay(d, k):
        asker = lax.rem(z + nz - (1 - 2 * d) * k, nz)
        return pltpu.make_async_copy(
            cache_ref.at[asker * NX + x], kv_buf.at[d, k - 1, x], kv_local.at[d, k - 1]
        )

    for j in range(NX):
        kv_copy(j % 2, depth, j).start()
    for k in range(depth - 1, reach, -1):
        for d in range(2):
            for j in range(NX):
                kv_copy(d, k, j).start()

    wide[...] = weight_ref[...].astype(jnp.float32)
    for part in range(4):
        w_parts[part] = wide[pl.ds(part, width, stride=4), :].astype(jnp.bfloat16)

    spread_mid(tok)
    for k in range(1, reach + 1):
        for d in range(2):
            kv_stay(d, k).start()
            for j in range(1, NX):
                kv_copy(d, k, j).start()
    home_stay().start()
    for j in range(1, NX):
        home_copy(j).start()

    ids = lax.broadcasted_iota(jnp.int32, (1, 128), 1)
    filled = jnp.clip(length_ref[0] - ids * PAGE, 0, PAGE).astype(jnp.float32)
    slot_of = keeper_ref[...] * 2 + slot_ref[...]
    filled_t = jnp.transpose(jnp.broadcast_to(filled, (128, 128)))
    slot_t = jnp.transpose(jnp.broadcast_to(slot_of.astype(jnp.float32), (128, 128)))
    lanes_f = lax.broadcasted_iota(jnp.int32, (128, 128), 1).astype(jnp.float32)
    slot_fill = jnp.sum(jnp.where(slot_t == lanes_f, filled_t, 0.0), axis=0, keepdims=True)
    fill_own[...] = jnp.broadcast_to(slot_fill, (8, 128))

    gain_f = gain_ref[...].astype(jnp.float32)
    gain_row = jnp.concatenate([gain_f[i : i + 1, :] for i in range(width // 128)], axis=1)

    def norm_block(block, g):
        x_f = block.astype(jnp.float32)
        mean = jnp.mean(x_f * x_f, axis=-1, keepdims=True)
        scaled = x_f * lax.rsqrt(mean + NORM_EPS) * gain_row
        normed[pl.ds(pl.multiple_of(g * rows, rows), rows), :] = scaled.astype(jnp.bfloat16)

    norm_block(tokens_ref[...], head)
    norm_block(tok_buf[left_head], left_head)
    norm_block(tok_buf[right_head], right_head)
    spread_late(tok)
    spread_begin(wout)
    norm_block(tok_buf[anti_head], anti_head)
    tok[0].wait_recv()
    norm_block(tok_buf[partner], partner)
    flip = lambda g: (g // CORES) * CORES + (1 - core)
    for i, g in ((7, left_head), (8, right_head)):
        tok[i].wait_recv()
        norm_block(tok_buf[flip(g)], flip(g))
    tok[9].wait_recv()
    tok[10].wait_recv()
    norm_block(tok_buf[flip(anti_head)], flip(anti_head))

    q_t = jnp.transpose(mm(normed[...], w_parts[0]))
    for h in range(chunks):
        q_own[h] = q_t[:, h * CHUNK : (h + 1) * CHUNK].astype(jnp.bfloat16)

    def q_copy(d, h, k):
        src = q_own.at[h] if isinstance(k, int) and k == 0 else q_buf.at[d, k - 1, h]
        return remote(
            src, q_buf.at[d, k, h], q_send.at[d, h, k], q_recv.at[d, h, k], ahead[d]
        )

    def q_done(d, h, k):
        place = q_buf.at[d, k, h]
        return remote(place, place, q_send.at[d, h, k], q_recv.at[d, h, k], ahead[d])

    def f_done(d, k):
        place = fill_buf.at[d, k]
        return remote(place, place, f_send.at[d, k], f_recv.at[d, k], ahead[d])

    def f_copy(d, k):
        src = fill_own if isinstance(k, int) and k == 0 else fill_buf.at[d, k - 1]
        return remote(src, fill_buf.at[d, k], f_send.at[d, k], f_recv.at[d, k], ahead[d])

    for d in range(2):
        f_copy(d, 0).start()
        for h in range(chunks):
            q_copy(d, h, 0).start()

    def unit_columns(v):
        return v * lax.rsqrt(jnp.sum(v * v, axis=0, keepdims=True) + UNIT_EPS)

    k_bf = mm(normed[...], w_parts[1]).astype(jnp.bfloat16)
    keys_own[...] = k_bf
    k_f = k_bf.astype(jnp.float32)
    k_unit = k_f * lax.rsqrt(jnp.sum(k_f * k_f, axis=-1, keepdims=True) + UNIT_EPS)
    v_bf = mm(normed[...], w_parts[2]).astype(jnp.bfloat16)
    v_t = jnp.transpose(v_bf.astype(jnp.float32))
    k_unit_t = jnp.transpose(k_unit)
    gates = jnp.transpose(mm(normed[...], w_parts[3]))
    values_t[...] = v_t.astype(jnp.bfloat16)
    units = unit_columns(q_t.astype(jnp.bfloat16).astype(jnp.float32))
    for b in range(prefill // BLK):
        key_unit[b] = k_unit[b * BLK : (b + 1) * BLK, :]
    for p in range(prefill // (2 * BLK)):
        columns = slice(p * 2 * BLK, (p + 1) * 2 * BLK)
        key_unit_t[p] = k_unit_t[:, columns]
        value_f[p] = v_t[:, columns]
        query_unit_t[p] = units[:, columns]
        gate_t[p] = gates[:, columns]
    mem_m[...] = state_ref[0]
    mem_s[...] = state_ref[1]

    def pick(blocks):
        count = len(blocks) * span
        for s, block in enumerate(blocks):
            kv_wide[s * span : (s + 1) * span, :] = block.astype(jnp.float32)
        keys = kv_wide[pl.ds(0, count // 2, stride=2), :].astype(jnp.bfloat16)
        vals = jnp.transpose(kv_wide[pl.ds(1, count // 2, stride=2), :]).astype(jnp.bfloat16)
        return keys, vals

    def split_near(d, k):
        kv_stay(d, k).wait()
        for j in range(1, NX):
            kv_copy(d, k, j).wait_recv()
        return pick([kv_buf[d, k - 1, s] for s in range(NX)])

    far_rows = (beyond + 1) * plane - plane // 2

    def split_far(d, k):
        if k == reach:
            keys, vals = split_near(d, k)
        elif k < depth:
            for j in range(NX):
                kv_copy(d, k, j).wait_recv()
            keys, vals = pick([kv_buf[d, k - 1, s] for s in range(NX)])
        else:
            for j in range(d, NX, 2):
                kv_copy(d, k, j).wait_recv()
            first = lax.rem(x + d, 2)
            keys, vals = pick([kv_buf[d, k - 1, first + s] for s in range(0, NX, 2)])
        at = (k - reach) * plane
        keys_far[d, at : at + keys.shape[0], :] = keys
        values_far[d, :, at : at + keys.shape[0]] = vals

    def bias_of(fill_row, base, count, skip=0):
        row_id = lax.broadcasted_iota(jnp.int32, (count, 128), 0)
        lane_id = lax.broadcasted_iota(jnp.int32, (count, 128), 1)
        slot_mine = lane_id == base + row_id // PAGE + skip * (row_id // (2 * PAGE))
        fills = jnp.sum(jnp.where(slot_mine, fill_row, 0.0), axis=1, keepdims=True)
        in_page = lax.rem(row_id[:, 0:1], PAGE).astype(jnp.float32)
        return jnp.where(in_page < fills, 0.0, NEG)

    def attend(keys, vals, bias, q):
        top, total, grown = soften(mm(keys, q) * scale + bias)
        return top, total, mm(vals, grown)

    def absorb(d, k):
        keys, vals = split_near(d, k)
        bias = bias_of(fill_buf[d, k - 1][0:1, :], z * (NX * 2), plane)
        for h in range(0, chunks, 2):
            q = jnp.concatenate([q_buf[d, k - 1, h], q_buf[d, k - 1, h + 1]], axis=1)
            top, total, acc = attend(keys, vals, bias, q)
            for u in range(2):
                columns = slice(u * CHUNK, (u + 1) * CHUNK)
                part_acc[d, k - 1, h + u] = acc[:, columns]
                part_ml[d, k - 1, h + u, 0:1, :] = top[:, columns]
                part_ml[d, k - 1, h + u, 1:2, :] = total[:, columns]

    def memory_pair(p):
        reads = []
        for u in range(2):
            columns = slice(u * BLK, (u + 1) * BLK)
            b = 2 * p + u
            state = mem_m[...]
            reads.append(exact(state, query_unit_t[p][:, columns]))
            errors = exact(state, key_unit_t[p][:, columns]) - value_f[p][:, columns]
            grads = exact(errors, key_unit[b])
            push = momentum_ref[0, 0] * mem_s[...] - stride_ref[0, 0] * grads
            keep = retention_ref[0, 0] * jnp.where(halving_ref[0, b] == 1, 0.5, 1.0)
            mem_s[...] = push
            mem_m[...] = keep * state + push
        extra_t[p] = jax.nn.sigmoid(gate_t[p]) * jnp.concatenate(reads, axis=1)

    def own_attention():
        home_stay().wait()
        for j in range(1, NX):
            home_copy(j).wait_recv()
        keys0, vals0 = pick([kv_home[s] for s in range(NX)])
        bias0 = bias_of(fill_own[0:1, :], z * (NX * 2), plane)
        persist_t = jnp.transpose(persist_ref[1].astype(jnp.float32)).astype(jnp.bfloat16)
        for h in range(chunks):
            count = (h + 1) * CHUNK
            q = q_own[h]
            s_c = mm(keys0, q) * scale + bias0
            s_p = mm(persist_ref[0], q) * scale
            s_t = mm(keys_own[0:count, :], q) * scale
            order = lax.broadcasted_iota(jnp.int32, (count, CHUNK), 0)
            place = lax.broadcasted_iota(jnp.int32, (count, CHUNK), 1) + h * CHUNK
            s_t = jnp.where(order <= place, s_t, NEG)
            top_c, total_c, grown_c = soften(s_c)
            top_t, total_t, grown_t = soften(s_t)
            top_p, total_p, grown_p = soften(s_p)
            top = jnp.maximum(jnp.maximum(top_c, top_t), top_p)
            e_c, e_t, e_p = jnp.exp(top_c - top), jnp.exp(top_t - top), jnp.exp(top_p - top)
            acc = mm(vals0, grown_c) * e_c + mm(values_t[:, 0:count], grown_t) * e_t
            home_acc[h] = acc + mm(persist_t, grown_p) * e_p
            home_ml[h, 0:1, :] = top
            home_ml[h, 1:2, :] = total_c * e_c + total_t * e_t + total_p * e_p

    def gather_step(k):
        for d in range(2):
            f_done(d, k - 1).wait_recv()
            f_copy(d, k).start()
            for h in range(chunks):
                q_done(d, h, k - 1).wait_recv()
                q_copy(d, h, k).start()

    far_ks = list(range(depth, reach, -1))
    for k in range(1, reach):
        gather_step(k)
        for d in range(2):
            absorb(d, k)
        if k > 1:
            for far_k in far_ks[k - 2 : k - 1] if k < reach - 1 else far_ks[k - 2 :]:
                for d in range(2):
                    split_far(d, far_k)
    spread_mid(wout)

    def ring_copies(d, h, k):
        return (
            remote(
                send_acc.at[d, k, h],
                recv_acc.at[d, k, h],
                a_send.at[d, h, k],
                a_recv.at[d, h, k],
                ahead[1 - d],
            ),
            remote(
                send_ml.at[d, k, h],
                recv_ml.at[d, k, h],
                m_send.at[d, h, k],
                m_recv.at[d, h, k],
                ahead[1 - d],
            ),
        )

    def ring_send(d, h, k, acc, top, total):
        send_acc[d, k, h] = acc.astype(jnp.bfloat16)
        send_ml[d, k, h, 0:1, :] = top
        send_ml[d, k, h, 1:2, :] = total
        for c in ring_copies(d, h, k):
            c.start()

    def join(first, second):
        top = jnp.maximum(first[1], second[1])
        e_a, e_b = jnp.exp(first[1] - top), jnp.exp(second[1] - top)
        return first[0] * e_a + second[0] * e_b, top, first[2] * e_a + second[2] * e_b

    def received(d, h, k):
        for c in ring_copies(d, h, k):
            c.wait_recv()
        return (
            recv_acc[d, k, h].astype(jnp.float32),
            recv_ml[d, k, h, 0:1, :],
            recv_ml[d, k, h, 1:2, :],
        )

    def partial(d, h, k):
        return part_acc[d, k, h], part_ml[d, k, h, 0:1, :], part_ml[d, k, h, 1:2, :]

    def ring_join(d, h, k):
        ring_send(d, h, k, *join(partial(d, h, k), received(d, h, k + 1)))

    last = reach - 1
    for d in range(2):
        split_far(d, reach)
    biases = []
    for d in range(2):
        f_done(d, last).wait_recv()
        fill_row = fill_buf[d, last][0:1, :]
        pieces = []
        for hop in range(beyond + 1):
            server = lax.rem(z + nz + (1 - 2 * d) * hop, nz)
            if hop < beyond:
                pieces.append(bias_of(fill_row, server * (NX * 2), plane))
            else:
                base = server * (NX * 2) + 2 * lax.rem(x + d, 2)
                pieces.append(bias_of(fill_row, base, plane // 2, 2))
        biases.append(jnp.concatenate(pieces, axis=0))
    for h in range(chunks):
        for d in range(2):
            q_done(d, h, last).wait_recv()
            top, total, acc = attend(
                keys_far[d], values_far[d], biases[d], q_buf[d, last, h]
            )
            ring_send(d, h, last, acc, top, total)

    own_attention()
    spread_late(wout)
    pairs = prefill // (2 * BLK)

    def ring_loop(i, carry):
        for h in range(chunks):
            for d in range(2):
                ring_join(d, h, last - i)
        pl.when(i <= pairs)(lambda: memory_pair(i - 1))
        return carry

    lax.fori_loop(1, reach, ring_loop, 0)
    for p in range(reach - 1, pairs):
        memory_pair(p)
    new_state_ref[0] = mem_m[...]
    new_state_ref[1] = mem_s[...]

    def head_copy(g):
        return remote(hout_buf.at[g], hrecv.at[head], h_send.at[g], h_recv.at[head], (req, g))

    def head_arrival(g):
        return remote(hout_buf.at[g], hrecv.at[g], h_send.at[g], h_recv.at[g], (req, g))

    per = heads // chunks
    for h in range(chunks):
        mine = home_acc[h], home_ml[h, 0:1, :], home_ml[h, 1:2, :]
        for d in range(2):
            mine = join(mine, received(d, h, 0))
        attended = mine[0] / mine[2]
        mean = jnp.mean(attended * attended, axis=0, keepdims=True)
        out = attended * lax.rsqrt(mean + UNIT_EPS) + extra_t[h]
        turned = jnp.transpose(out).astype(jnp.bfloat16)
        for g in range(h * per, (h + 1) * per):
            hout_buf[g] = turned[(g - h * per) * rows : (g - h * per + 1) * rows, :]
        for g in range(h * per, (h + 1) * per):
            pl.when(g != head)(lambda g=g: head_copy(g).start())

    for i in (0, 7, 8, 9, 10):
        wout[i].wait_recv()
    layer = mm(hout_buf[head], out_weight_ref[...]).astype(jnp.bfloat16).astype(jnp.float32)
    for j in range(1, heads):
        group = lax.rem(head + j, heads)
        head_arrival(group).wait_recv()
        layer = layer + mm(hrecv[group], wout_buf[group]).astype(jnp.bfloat16).astype(jnp.float32)
    layer_ref[...] = layer.astype(jnp.bfloat16)

    for c in tok + wout:
        c.wait_send()
    for j in range(1, heads):
        head_copy(lax.rem(head + j, heads)).wait_send()
    for j in range(1, NX):
        home_copy(j).wait_send()
        for k in range(1, reach + 1):
            for d in range(2):
                kv_copy(d, k, j).wait_send()
    for j in range(NX):
        for k in range(reach + 1, depth):
            for d in range(2):
                kv_copy(d, k, j).wait_send()
        kv_copy(j % 2, depth, j).wait_send()

    def ends(k, carry):
        for d in range(2):
            f_done(d, k).wait_send()
            for h in range(chunks):
                q_done(d, h, k).wait_send()
                for c in ring_copies(d, h, k):
                    c.wait_send()
        return carry

    lax.fori_loop(0, reach, ends, 0)


def settle(layer_ref, state_ref, layer_out, state_out):
    layer_out[...] = layer_ref[...]
    state_out[...] = state_ref[...]


def shards(
    tokens,
    gain,
    projection_weight,
    output_weight,
    persist,
    cache_page_slots,
    cached_length,
    page_keeper,
    page_slot_index,
    memory_state,
    retention,
    momentum,
    memory_step_scale,
    halving_updates,
    *,
    reqs,
    heads,
):
    nz, ny = reqs // NX, heads // CORES
    depth = nz // 2
    rows, width = tokens.shape[1], tokens.shape[2]
    prefill = rows * heads
    chunks = prefill // CHUNK
    half = CHUNK
    blocks = prefill // BLK
    span = cache_page_slots.shape[2] * 2
    bf, f32 = jnp.bfloat16, jnp.float32
    vmem = pl.BlockSpec(memory_space=pltpu.VMEM)
    smem = pl.BlockSpec(memory_space=pltpu.SMEM)
    hbm = pl.BlockSpec(memory_space=pl.ANY)
    sems = pltpu.SemaphoreType.DMA
    reach = min(REACH, depth - 1)
    pairs = blocks // 2
    rings = (2, reach, chunks)
    far_rows = (depth - reach + 1) * NX * span // 2 - NX * span // 4
    scratch = [
        pltpu.VMEM((heads, rows, width), bf),
        pltpu.VMEM((heads,) + output_weight.shape, bf),
        pltpu.VMEM((4 * width, HD), f32),
        pltpu.VMEM((4, width, HD), bf),
        pltpu.VMEM((prefill, width), bf),
        pltpu.VMEM((NX, span, HD), bf),
        pltpu.VMEM((2, depth, NX, span, HD), bf),
        pltpu.VMEM((chunks, HD, half), bf),
        pltpu.VMEM(rings + (HD, half), bf),
        pltpu.VMEM((8, 128), f32),
        pltpu.VMEM((2, reach, 8, 128), f32),
        pltpu.VMEM((prefill, HD), bf),
        pltpu.VMEM((HD, prefill), bf),
        pltpu.VMEM((blocks, BLK, HD), f32),
        pltpu.VMEM((pairs, HD, 2 * BLK), f32),
        pltpu.VMEM((pairs, HD, 2 * BLK), f32),
        pltpu.VMEM((pairs, HD, 2 * BLK), f32),
        pltpu.VMEM((pairs, HD, 2 * BLK), f32),
        pltpu.VMEM((pairs, HD, 2 * BLK), f32),
        pltpu.VMEM((HD, HD), f32),
        pltpu.VMEM((HD, HD), f32),
        pltpu.VMEM((NX * span, HD), f32),
        pltpu.VMEM((2, far_rows, HD), bf),
        pltpu.VMEM((2, HD, far_rows), bf),
        pltpu.VMEM(rings + (HD, half), f32),
        pltpu.VMEM(rings + (2, half), f32),
        pltpu.VMEM(rings + (HD, half), bf),
        pltpu.VMEM(rings + (2, half), f32),
        pltpu.VMEM(rings + (HD, half), bf),
        pltpu.VMEM(rings + (2, half), f32),
        pltpu.VMEM((chunks, HD, half), f32),
        pltpu.VMEM((chunks, 2, half), f32),
        pltpu.VMEM((heads, rows, HD), bf),
        pltpu.VMEM((heads, rows, HD), bf),
        sems((11,)),
        sems((11,)),
        sems((11,)),
        sems((11,)),
        sems((NX,)),
        sems((NX,)),
        sems,
        sems((2, depth, NX)),
        sems((2, depth, NX)),
        sems((2, depth)),
        sems((2, chunks, reach)),
        sems((2, chunks, reach)),
        sems((2, reach)),
        sems((2, reach)),
        sems((2, chunks, reach)),
        sems((2, chunks, reach)),
        sems((2, chunks, reach)),
        sems((2, chunks, reach)),
        sems((heads,)),
        sems((heads,)),
    ]
    layer, state = pl.pallas_call(
        functools.partial(kernel, nz, ny),
        out_shape=(
            jax.ShapeDtypeStruct((rows, width), bf),
            jax.ShapeDtypeStruct((2, HD, HD), f32),
        ),
        in_specs=[vmem] * 5 + [hbm, smem, vmem, vmem, vmem] + [smem] * 4,
        out_specs=(vmem, vmem),
        scratch_shapes=scratch,
        compiler_params=pltpu.CompilerParams(
            collective_id=0, has_side_effects=True, vmem_limit_bytes=56 * 1024 * 1024
        ),
    )(
        tokens.reshape(rows, width),
        gain.reshape(width // 128, 128),
        projection_weight.reshape(4 * width, HD),
        output_weight,
        persist,
        cache_page_slots.reshape(cache_page_slots.shape[1], span, HD),
        cached_length,
        page_keeper,
        page_slot_index,
        memory_state.reshape(2, HD, HD),
        retention,
        momentum,
        memory_step_scale,
        halving_updates,
    )
    layer, state = pl.pallas_call(
        settle,
        out_shape=(
            jax.ShapeDtypeStruct((rows, width), bf),
            jax.ShapeDtypeStruct((2, HD, HD), f32),
        ),
        in_specs=[vmem, vmem],
        out_specs=(vmem, vmem),
    )(layer, state)
    return layer.reshape(tokens.shape), state.reshape(memory_state.shape)


def solution(mesh):
    in_specs = (
        P("req", "head", None),
        P(),
        P(None, None, "head"),
        P("head", None),
        P(None, None, "head"),
        P("req", None, None, None, "head"),
        P("req"),
        P("req", None),
        P("req", None),
        P(None, "req", "head", None, None),
        P("req", "head"),
        P("req", "head"),
        P("req", "head"),
        P("req", None),
    )
    out_specs = (P("req", "head", None), P(None, "req", "head", None, None))
    body = functools.partial(shards, reqs=mesh.shape["req"], heads=mesh.shape["head"])
    return jax.shard_map(body, mesh=mesh, in_specs=in_specs, out_specs=out_specs, check_vma=False)
```

```python
import functools
import math

import jax
import jax.numpy as jnp
from jax import lax
from jax.experimental import pallas as pl
from jax.experimental.pallas import tpu as pltpu
from jax.sharding import PartitionSpec as P

HD = 128
BLK = 64
PAGE = 32
NX = 4
CORES = 2
REACH = 5
CHUNK = 128
MESH = pl.DeviceIdType.MESH
NEG = -1e30
FLOOR = -5e29
NORM_EPS = 1e-05
UNIT_EPS = 1e-06
HIGHEST = lax.Precision.HIGHEST


def mm(left, right):
    return jnp.dot(left, right, preferred_element_type=jnp.float32)


def exact(left, right):
    return jnp.dot(left, right, precision=HIGHEST, preferred_element_type=jnp.float32)


def soften(scores):
    top = jnp.maximum(jnp.max(scores, axis=0, keepdims=True), FLOOR)
    grown = jnp.exp(scores - top)
    return top, jnp.sum(grown, axis=0, keepdims=True), grown.astype(jnp.bfloat16)


def kernel(
    nz,
    ny,
    tokens_ref,
    gain_ref,
    weight_ref,
    out_weight_ref,
    persist_ref,
    cache_ref,
    length_ref,
    keeper_ref,
    slot_ref,
    state_ref,
    retention_ref,
    momentum_ref,
    stride_ref,
    halving_ref,
    layer_ref,
    new_state_ref,
    tok_buf,
    wout_buf,
    wide,
    w_parts,
    normed,
    kv_home,
    kv_buf,
    q_own,
    q_buf,
    fill_own,
    fill_buf,
    keys_own,
    values_t,
    key_unit,
    key_unit_t,
    value_f,
    query_unit_t,
    gate_t,
    extra_t,
    mem_m,
    mem_s,
    kv_wide,
    keys_far,
    values_far,
    part_acc,
    part_ml,
    send_acc,
    send_ml,
    recv_acc,
    recv_ml,
    home_acc,
    home_ml,
    hout_buf,
    hrecv,
    tok_send,
    tok_recv,
    wo_send,
    wo_recv,
    h0_send,
    h0_recv,
    h0_local,
    kv_send,
    kv_recv,
    kv_local,
    q_send,
    q_recv,
    f_send,
    f_recv,
    a_send,
    a_recv,
    m_send,
    m_recv,
    h_send,
    h_recv,
):
    req = lax.axis_index("req")
    head = lax.axis_index("head")
    z, x = req // NX, lax.rem(req, NX)
    y, core = head // CORES, lax.rem(head, CORES)
    heads = ny * CORES
    rows = tokens_ref.shape[0]
    prefill = heads * rows
    chunks = prefill // CHUNK
    width = tokens_ref.shape[1]
    span = cache_ref.shape[1]
    plane = NX * span // 2
    depth = nz // 2
    reach = min(REACH, depth - 1)
    beyond = depth - reach
    scale = 1.0 / math.sqrt(HD)

    partner = y * CORES + (1 - core)
    right_head = lax.rem(y + 1, ny) * CORES + core
    left_head = lax.rem(y + ny - 1, ny) * CORES + core
    anti_head = lax.rem(y + 2, ny) * CORES + core
    z_next = (lax.rem(z + 1, nz) * NX + x, head)
    z_back = (lax.rem(z + nz - 1, nz) * NX + x, head)
    ahead = (z_next, z_back)

    barrier = pltpu.get_barrier_semaphore()
    for hop in range(-beyond, beyond + 1):
        for j in range(NX):
            if hop or j:
                peer = (lax.rem(z + nz + hop, nz) * NX + lax.rem(x + j, NX), head)
                pl.semaphore_signal(barrier, inc=1, device_id=peer, device_id_type=MESH)
    for j in range(1, heads):
        peer = (req, lax.rem(head + j, heads))
        pl.semaphore_signal(barrier, inc=1, device_id=peer, device_id_type=MESH)
    pl.semaphore_wait(barrier, (2 * beyond + 1) * NX - 1 + heads - 1)

    def remote(src, dst, send, recv, device):
        return pltpu.make_async_remote_copy(
            src_ref=src,
            dst_ref=dst,
            send_sem=send,
            recv_sem=recv,
            device_id=device,
            device_id_type=MESH,
        )

    def spread(own, buf, send, recv):
        cut = own.shape[0] // 2
        low, high = pl.ds(0, cut), pl.ds(cut, cut)
        to = lambda src, dst, i, g: remote(src, dst, send.at[i], recv.at[i], (req, g))
        from_left = buf.at[left_head]
        from_right = buf.at[right_head]
        mine = buf.at[head]
        return (
            to(own, mine, 0, partner),
            to(own.at[low], buf.at[head, low], 1, right_head),
            to(own.at[high], buf.at[head, high], 2, right_head),
            to(own.at[low], buf.at[head, low], 3, left_head),
            to(own.at[high], buf.at[head, high], 4, left_head),
            to(buf.at[left_head, low], buf.at[left_head, low], 5, right_head),
            to(buf.at[right_head, high], buf.at[right_head, high], 6, left_head),
            to(from_left, from_left, 7, partner),
            to(from_right, from_right, 8, partner),
            to(buf.at[anti_head, low], buf.at[anti_head, low], 9, partner),
            to(buf.at[anti_head, high], buf.at[anti_head, high], 10, partner),
        )

    def spread_begin(c):
        for i in (1, 4, 0, 2, 3):
            c[i].start()

    def spread_mid(c):
        for first, then in ((1, 5), (4, 6), (2, 7), (3, 8)):
            c[first].wait_recv()
            c[then].start()

    def spread_late(c):
        for first, then in ((5, 9), (6, 10)):
            c[first].wait_recv()
            c[then].start()

    tok = spread(tokens_ref, tok_buf, tok_send, tok_recv)
    wout = spread(out_weight_ref, wout_buf, wo_send, wo_recv)
    spread_begin(tok)

    def home_copy(j):
        to_x = lax.rem(x + j, NX)
        return remote(
            cache_ref.at[z * NX + to_x],
            kv_home.at[x],
            h0_send.at[j],
            h0_recv.at[j],
            (z * NX + to_x, head),
        )

    def home_stay():
        return pltpu.make_async_copy(cache_ref.at[req], kv_home.at[x], h0_local)

    def kv_copy(d, k, j):
        sign = 1 - 2 * d
        to_x = lax.rem(x + j, NX)
        asker = lax.rem(z + nz - sign * k, nz)
        over = max(k - reach, 0) if isinstance(k, int) else 0
        server = lax.rem(z + nz - sign * over, nz)
        return remote(
            cache_ref.at[asker * NX + to_x],
            kv_buf.at[d, k - 1, x],
            kv_send.at[d, k - 1, j],
            kv_recv.at[d, k - 1, j],
            (server * NX + to_x, head),
        )

    def kv_stay(d, k):
        asker = lax.rem(z + nz - (1 - 2 * d) * k, nz)
        return pltpu.make_async_copy(
            cache_ref.at[asker * NX + x], kv_buf.at[d, k - 1, x], kv_local.at[d, k - 1]
        )

    for j in range(NX):
        kv_copy(j % 2, depth, j).start()
    for k in range(depth - 1, reach, -1):
        for d in range(2):
            for j in range(NX):
                kv_copy(d, k, j).start()

    wide[...] = weight_ref[...].astype(jnp.float32)
    for part in range(4):
        w_parts[part] = wide[pl.ds(part, width, stride=4), :].astype(jnp.bfloat16)

    spread_mid(tok)
    for k in range(1, reach + 1):
        if k == reach - 1:
            home_stay().start()
            for j in range(1, NX):
                home_copy(j).start()
        for d in range(2):
            kv_stay(d, k).start()
            for j in range(1, NX):
                kv_copy(d, k, j).start()

    ids = lax.broadcasted_iota(jnp.int32, (1, 128), 1)
    filled = jnp.clip(length_ref[0] - ids * PAGE, 0, PAGE).astype(jnp.float32)
    slot_of = keeper_ref[...] * 2 + slot_ref[...]
    filled_t = jnp.transpose(jnp.broadcast_to(filled, (128, 128)))
    slot_t = jnp.transpose(jnp.broadcast_to(slot_of.astype(jnp.float32), (128, 128)))
    lanes_f = lax.broadcasted_iota(jnp.int32, (128, 128), 1).astype(jnp.float32)
    slot_fill = jnp.sum(jnp.where(slot_t == lanes_f, filled_t, 0.0), axis=0, keepdims=True)
    fill_own[...] = jnp.broadcast_to(slot_fill, (8, 128))

    gain_f = gain_ref[...].astype(jnp.float32)
    gain_row = jnp.concatenate([gain_f[i : i + 1, :] for i in range(width // 128)], axis=1)

    def norm_block(block, g):
        x_f = block.astype(jnp.float32)
        mean = jnp.mean(x_f * x_f, axis=-1, keepdims=True)
        scaled = x_f * lax.rsqrt(mean + NORM_EPS) * gain_row
        normed[pl.ds(pl.multiple_of(g * rows, rows), rows), :] = scaled.astype(jnp.bfloat16)

    norm_block(tokens_ref[...], head)
    norm_block(tok_buf[left_head], left_head)
    norm_block(tok_buf[right_head], right_head)
    spread_late(tok)
    spread_begin(wout)
    norm_block(tok_buf[anti_head], anti_head)
    tok[0].wait_recv()
    norm_block(tok_buf[partner], partner)
    flip = lambda g: (g // CORES) * CORES + (1 - core)
    for i, g in ((7, left_head), (8, right_head)):
        tok[i].wait_recv()
        norm_block(tok_buf[flip(g)], flip(g))
    tok[9].wait_recv()
    tok[10].wait_recv()
    norm_block(tok_buf[flip(anti_head)], flip(anti_head))

    q_t = jnp.transpose(mm(normed[...], w_parts[0]))
    for h in range(chunks):
        q_own[h] = q_t[:, h * CHUNK : (h + 1) * CHUNK].astype(jnp.bfloat16)

    def q_copy(d, h, k):
        src = q_own.at[h] if isinstance(k, int) and k == 0 else q_buf.at[d, k - 1, h]
        return remote(
            src, q_buf.at[d, k, h], q_send.at[d, h, k], q_recv.at[d, h, k], ahead[d]
        )

    def q_done(d, h, k):
        place = q_buf.at[d, k, h]
        return remote(place, place, q_send.at[d, h, k], q_recv.at[d, h, k], ahead[d])

    def f_done(d, k):
        place = fill_buf.at[d, k]
        return remote(place, place, f_send.at[d, k], f_recv.at[d, k], ahead[d])

    def f_copy(d, k):
        src = fill_own if isinstance(k, int) and k == 0 else fill_buf.at[d, k - 1]
        return remote(src, fill_buf.at[d, k], f_send.at[d, k], f_recv.at[d, k], ahead[d])

    for d in range(2):
        f_copy(d, 0).start()
        for h in range(chunks):
            q_copy(d, h, 0).start()

    def unit_columns(v):
        return v * lax.rsqrt(jnp.sum(v * v, axis=0, keepdims=True) + UNIT_EPS)

    k_bf = mm(normed[...], w_parts[1]).astype(jnp.bfloat16)
    keys_own[...] = k_bf
    k_f = k_bf.astype(jnp.float32)
    k_unit = k_f * lax.rsqrt(jnp.sum(k_f * k_f, axis=-1, keepdims=True) + UNIT_EPS)
    v_bf = mm(normed[...], w_parts[2]).astype(jnp.bfloat16)
    v_t = jnp.transpose(v_bf.astype(jnp.float32))
    k_unit_t = jnp.transpose(k_unit)
    gates = jnp.transpose(mm(normed[...], w_parts[3]))
    values_t[...] = v_t.astype(jnp.bfloat16)
    units = unit_columns(q_t.astype(jnp.bfloat16).astype(jnp.float32))
    for b in range(prefill // BLK):
        key_unit[b] = k_unit[b * BLK : (b + 1) * BLK, :]
    for p in range(prefill // (2 * BLK)):
        columns = slice(p * 2 * BLK, (p + 1) * 2 * BLK)
        key_unit_t[p] = k_unit_t[:, columns]
        value_f[p] = v_t[:, columns]
        query_unit_t[p] = units[:, columns]
        gate_t[p] = gates[:, columns]
    mem_m[...] = state_ref[0]
    mem_s[...] = state_ref[1]

    def pick(blocks):
        count = len(blocks) * span
        for s, block in enumerate(blocks):
            kv_wide[s * span : (s + 1) * span, :] = block.astype(jnp.float32)
        keys = kv_wide[pl.ds(0, count // 2, stride=2), :].astype(jnp.bfloat16)
        vals = jnp.transpose(kv_wide[pl.ds(1, count // 2, stride=2), :]).astype(jnp.bfloat16)
        return keys, vals

    def split_near(d, k):
        kv_stay(d, k).wait()
        for j in range(1, NX):
            kv_copy(d, k, j).wait_recv()
        return pick([kv_buf[d, k - 1, s] for s in range(NX)])

    far_rows = (beyond + 1) * plane - plane // 2

    def split_far(d, k):
        if k == reach:
            keys, vals = split_near(d, k)
        elif k < depth:
            for j in range(NX):
                kv_copy(d, k, j).wait_recv()
            keys, vals = pick([kv_buf[d, k - 1, s] for s in range(NX)])
        else:
            for j in range(d, NX, 2):
                kv_copy(d, k, j).wait_recv()
            first = lax.rem(x + d, 2)
            keys, vals = pick([kv_buf[d, k - 1, first + s] for s in range(0, NX, 2)])
        at = (k - reach) * plane
        keys_far[d, at : at + keys.shape[0], :] = keys
        values_far[d, :, at : at + keys.shape[0]] = vals

    def bias_of(fill_row, base, count, skip=0):
        row_id = lax.broadcasted_iota(jnp.int32, (count, 128), 0)
        lane_id = lax.broadcasted_iota(jnp.int32, (count, 128), 1)
        slot_mine = lane_id == base + row_id // PAGE + skip * (row_id // (2 * PAGE))
        fills = jnp.sum(jnp.where(slot_mine, fill_row, 0.0), axis=1, keepdims=True)
        in_page = lax.rem(row_id[:, 0:1], PAGE).astype(jnp.float32)
        return jnp.where(in_page < fills, 0.0, NEG)

    def attend(keys, vals, bias, q):
        top, total, grown = soften(mm(keys, q) * scale + bias)
        return top, total, mm(vals, grown)

    def absorb(d, k):
        keys, vals = split_near(d, k)
        bias = bias_of(fill_buf[d, k - 1][0:1, :], z * (NX * 2), plane)
        for h in range(0, chunks, 2):
            q = jnp.concatenate([q_buf[d, k - 1, h], q_buf[d, k - 1, h + 1]], axis=1)
            top, total, acc = attend(keys, vals, bias, q)
            for u in range(2):
                columns = slice(u * CHUNK, (u + 1) * CHUNK)
                part_acc[d, k - 1, h + u] = acc[:, columns]
                part_ml[d, k - 1, h + u, 0:1, :] = top[:, columns]
                part_ml[d, k - 1, h + u, 1:2, :] = total[:, columns]

    def memory_pair(p):
        reads = []
        for u in range(2):
            columns = slice(u * BLK, (u + 1) * BLK)
            b = 2 * p + u
            state = mem_m[...]
            reads.append(exact(state, query_unit_t[p][:, columns]))
            errors = exact(state, key_unit_t[p][:, columns]) - value_f[p][:, columns]
            grads = exact(errors, key_unit[b])
            push = momentum_ref[0, 0] * mem_s[...] - stride_ref[0, 0] * grads
            keep = retention_ref[0, 0] * jnp.where(halving_ref[0, b] == 1, 0.5, 1.0)
            mem_s[...] = push
            mem_m[...] = keep * state + push
        extra_t[p] = jax.nn.sigmoid(gate_t[p]) * jnp.concatenate(reads, axis=1)

    def own_attention():
        home_stay().wait()
        for j in range(1, NX):
            home_copy(j).wait_recv()
        keys0, vals0 = pick([kv_home[s] for s in range(NX)])
        bias0 = bias_of(fill_own[0:1, :], z * (NX * 2), plane)
        persist_t = jnp.transpose(persist_ref[1].astype(jnp.float32)).astype(jnp.bfloat16)
        for h in range(chunks):
            count = (h + 1) * CHUNK
            q = q_own[h]
            s_c = mm(keys0, q) * scale + bias0
            s_p = mm(persist_ref[0], q) * scale
            s_t = mm(keys_own[0:count, :], q) * scale
            order = lax.broadcasted_iota(jnp.int32, (count, CHUNK), 0)
            place = lax.broadcasted_iota(jnp.int32, (count, CHUNK), 1) + h * CHUNK
            s_t = jnp.where(order <= place, s_t, NEG)
            top_c, total_c, grown_c = soften(s_c)
            top_t, total_t, grown_t = soften(s_t)
            top_p, total_p, grown_p = soften(s_p)
            top = jnp.maximum(jnp.maximum(top_c, top_t), top_p)
            e_c, e_t, e_p = jnp.exp(top_c - top), jnp.exp(top_t - top), jnp.exp(top_p - top)
            acc = mm(vals0, grown_c) * e_c + mm(values_t[:, 0:count], grown_t) * e_t
            home_acc[h] = acc + mm(persist_t, grown_p) * e_p
            home_ml[h, 0:1, :] = top
            home_ml[h, 1:2, :] = total_c * e_c + total_t * e_t + total_p * e_p

    def gather_step(k):
        for d in range(2):
            f_done(d, k - 1).wait_recv()
            f_copy(d, k).start()
            for h in range(chunks):
                q_done(d, h, k - 1).wait_recv()
                q_copy(d, h, k).start()

    far_ks = list(range(depth, reach, -1))
    for k in range(1, reach):
        gather_step(k)
        for d in range(2):
            absorb(d, k)
        if k > 1:
            for far_k in far_ks[k - 2 : k - 1] if k < reach - 1 else far_ks[k - 2 :]:
                for d in range(2):
                    split_far(d, far_k)
        if k == reach - 2:
            own_attention()
    spread_mid(wout)

    def ring_copies(d, h, k):
        return (
            remote(
                send_acc.at[d, k, h],
                recv_acc.at[d, k, h],
                a_send.at[d, h, k],
                a_recv.at[d, h, k],
                ahead[1 - d],
            ),
            remote(
                send_ml.at[d, k, h],
                recv_ml.at[d, k, h],
                m_send.at[d, h, k],
                m_recv.at[d, h, k],
                ahead[1 - d],
            ),
        )

    def ring_send(d, h, k, acc, top, total):
        send_acc[d, k, h] = acc.astype(jnp.bfloat16)
        send_ml[d, k, h, 0:1, :] = top
        send_ml[d, k, h, 1:2, :] = total
        for c in ring_copies(d, h, k):
            c.start()

    def join(first, second):
        top = jnp.maximum(first[1], second[1])
        e_a, e_b = jnp.exp(first[1] - top), jnp.exp(second[1] - top)
        return first[0] * e_a + second[0] * e_b, top, first[2] * e_a + second[2] * e_b

    def received(d, h, k):
        for c in ring_copies(d, h, k):
            c.wait_recv()
        return (
            recv_acc[d, k, h].astype(jnp.float32),
            recv_ml[d, k, h, 0:1, :],
            recv_ml[d, k, h, 1:2, :],
        )

    def partial(d, h, k):
        return part_acc[d, k, h], part_ml[d, k, h, 0:1, :], part_ml[d, k, h, 1:2, :]

    def ring_join(d, h, k):
        ring_send(d, h, k, *join(partial(d, h, k), received(d, h, k + 1)))

    last = reach - 1
    for d in range(2):
        split_far(d, reach)
    biases = []
    for d in range(2):
        f_done(d, last).wait_recv()
        fill_row = fill_buf[d, last][0:1, :]
        pieces = []
        for hop in range(beyond + 1):
            server = lax.rem(z + nz + (1 - 2 * d) * hop, nz)
            if hop < beyond:
                pieces.append(bias_of(fill_row, server * (NX * 2), plane))
            else:
                base = server * (NX * 2) + 2 * lax.rem(x + d, 2)
                pieces.append(bias_of(fill_row, base, plane // 2, 2))
        biases.append(jnp.concatenate(pieces, axis=0))
    for h in range(chunks):
        for d in range(2):
            q_done(d, h, last).wait_recv()
            top, total, acc = attend(
                keys_far[d], values_far[d], biases[d], q_buf[d, last, h]
            )
            ring_send(d, h, last, acc, top, total)

    spread_late(wout)
    pairs = prefill // (2 * BLK)

    def ring_loop(i, carry):
        for h in range(chunks):
            for d in range(2):
                ring_join(d, h, last - i)
        pl.when(i <= pairs)(lambda: memory_pair(i - 1))
        return carry

    lax.fori_loop(1, reach, ring_loop, 0)
    for p in range(reach - 1, pairs):
        memory_pair(p)
    new_state_ref[0] = mem_m[...]
    new_state_ref[1] = mem_s[...]

    def head_copy(g):
        return remote(hout_buf.at[g], hrecv.at[head], h_send.at[g], h_recv.at[head], (req, g))

    def head_arrival(g):
        return remote(hout_buf.at[g], hrecv.at[g], h_send.at[g], h_recv.at[g], (req, g))

    per = heads // chunks
    for h in range(chunks):
        mine = home_acc[h], home_ml[h, 0:1, :], home_ml[h, 1:2, :]
        for d in range(2):
            mine = join(mine, received(d, h, 0))
        attended = mine[0] / mine[2]
        mean = jnp.mean(attended * attended, axis=0, keepdims=True)
        out = attended * lax.rsqrt(mean + UNIT_EPS) + extra_t[h]
        turned = jnp.transpose(out).astype(jnp.bfloat16)
        for g in range(h * per, (h + 1) * per):
            hout_buf[g] = turned[(g - h * per) * rows : (g - h * per + 1) * rows, :]
        for g in range(h * per, (h + 1) * per):
            pl.when(g != head)(lambda g=g: head_copy(g).start())

    for i in (0, 7, 8, 9, 10):
        wout[i].wait_recv()
    layer = mm(hout_buf[head], out_weight_ref[...]).astype(jnp.bfloat16).astype(jnp.float32)
    for j in range(1, heads):
        group = lax.rem(head + j, heads)
        head_arrival(group).wait_recv()
        layer = layer + mm(hrecv[group], wout_buf[group]).astype(jnp.bfloat16).astype(jnp.float32)
    layer_ref[...] = layer.astype(jnp.bfloat16)

    for c in tok + wout:
        c.wait_send()
    for j in range(1, heads):
        head_copy(lax.rem(head + j, heads)).wait_send()
    for j in range(1, NX):
        home_copy(j).wait_send()
        for k in range(1, reach + 1):
            for d in range(2):
                kv_copy(d, k, j).wait_send()
    for j in range(NX):
        for k in range(reach + 1, depth):
            for d in range(2):
                kv_copy(d, k, j).wait_send()
        kv_copy(j % 2, depth, j).wait_send()

    def ends(k, carry):
        for d in range(2):
            f_done(d, k).wait_send()
            for h in range(chunks):
                q_done(d, h, k).wait_send()
                for c in ring_copies(d, h, k):
                    c.wait_send()
        return carry

    lax.fori_loop(0, reach, ends, 0)


def settle(layer_ref, state_ref, layer_out, state_out):
    layer_out[...] = layer_ref[...]
    state_out[...] = state_ref[...]


def shards(
    tokens,
    gain,
    projection_weight,
    output_weight,
    persist,
    cache_page_slots,
    cached_length,
    page_keeper,
    page_slot_index,
    memory_state,
    retention,
    momentum,
    memory_step_scale,
    halving_updates,
    *,
    reqs,
    heads,
):
    nz, ny = reqs // NX, heads // CORES
    depth = nz // 2
    rows, width = tokens.shape[1], tokens.shape[2]
    prefill = rows * heads
    chunks = prefill // CHUNK
    half = CHUNK
    blocks = prefill // BLK
    span = cache_page_slots.shape[2] * 2
    bf, f32 = jnp.bfloat16, jnp.float32
    vmem = pl.BlockSpec(memory_space=pltpu.VMEM)
    smem = pl.BlockSpec(memory_space=pltpu.SMEM)
    hbm = pl.BlockSpec(memory_space=pl.ANY)
    sems = pltpu.SemaphoreType.DMA
    reach = min(REACH, depth - 1)
    pairs = blocks // 2
    rings = (2, reach, chunks)
    far_rows = (depth - reach + 1) * NX * span // 2 - NX * span // 4
    scratch = [
        pltpu.VMEM((heads, rows, width), bf),
        pltpu.VMEM((heads,) + output_weight.shape, bf),
        pltpu.VMEM((4 * width, HD), f32),
        pltpu.VMEM((4, width, HD), bf),
        pltpu.VMEM((prefill, width), bf),
        pltpu.VMEM((NX, span, HD), bf),
        pltpu.VMEM((2, depth, NX, span, HD), bf),
        pltpu.VMEM((chunks, HD, half), bf),
        pltpu.VMEM(rings + (HD, half), bf),
        pltpu.VMEM((8, 128), f32),
        pltpu.VMEM((2, reach, 8, 128), f32),
        pltpu.VMEM((prefill, HD), bf),
        pltpu.VMEM((HD, prefill), bf),
        pltpu.VMEM((blocks, BLK, HD), f32),
        pltpu.VMEM((pairs, HD, 2 * BLK), f32),
        pltpu.VMEM((pairs, HD, 2 * BLK), f32),
        pltpu.VMEM((pairs, HD, 2 * BLK), f32),
        pltpu.VMEM((pairs, HD, 2 * BLK), f32),
        pltpu.VMEM((pairs, HD, 2 * BLK), f32),
        pltpu.VMEM((HD, HD), f32),
        pltpu.VMEM((HD, HD), f32),
        pltpu.VMEM((NX * span, HD), f32),
        pltpu.VMEM((2, far_rows, HD), bf),
        pltpu.VMEM((2, HD, far_rows), bf),
        pltpu.VMEM(rings + (HD, half), f32),
        pltpu.VMEM(rings + (2, half), f32),
        pltpu.VMEM(rings + (HD, half), bf),
        pltpu.VMEM(rings + (2, half), f32),
        pltpu.VMEM(rings + (HD, half), bf),
        pltpu.VMEM(rings + (2, half), f32),
        pltpu.VMEM((chunks, HD, half), f32),
        pltpu.VMEM((chunks, 2, half), f32),
        pltpu.VMEM((heads, rows, HD), bf),
        pltpu.VMEM((heads, rows, HD), bf),
        sems((11,)),
        sems((11,)),
        sems((11,)),
        sems((11,)),
        sems((NX,)),
        sems((NX,)),
        sems,
        sems((2, depth, NX)),
        sems((2, depth, NX)),
        sems((2, depth)),
        sems((2, chunks, reach)),
        sems((2, chunks, reach)),
        sems((2, reach)),
        sems((2, reach)),
        sems((2, chunks, reach)),
        sems((2, chunks, reach)),
        sems((2, chunks, reach)),
        sems((2, chunks, reach)),
        sems((heads,)),
        sems((heads,)),
    ]
    layer, state = pl.pallas_call(
        functools.partial(kernel, nz, ny),
        out_shape=(
            jax.ShapeDtypeStruct((rows, width), bf),
            jax.ShapeDtypeStruct((2, HD, HD), f32),
        ),
        in_specs=[vmem] * 5 + [hbm, smem, vmem, vmem, vmem] + [smem] * 4,
        out_specs=(vmem, vmem),
        scratch_shapes=scratch,
        compiler_params=pltpu.CompilerParams(
            collective_id=0, has_side_effects=True, vmem_limit_bytes=56 * 1024 * 1024
        ),
    )(
        tokens.reshape(rows, width),
        gain.reshape(width // 128, 128),
        projection_weight.reshape(4 * width, HD),
        output_weight,
        persist,
        cache_page_slots.reshape(cache_page_slots.shape[1], span, HD),
        cached_length,
        page_keeper,
        page_slot_index,
        memory_state.reshape(2, HD, HD),
        retention,
        momentum,
        memory_step_scale,
        halving_updates,
    )
    layer, state = pl.pallas_call(
        settle,
        out_shape=(
            jax.ShapeDtypeStruct((rows, width), bf),
            jax.ShapeDtypeStruct((2, HD, HD), f32),
        ),
        in_specs=[vmem, vmem],
        out_specs=(vmem, vmem),
    )(layer, state)
    return layer.reshape(tokens.shape), state.reshape(memory_state.shape)


def solution(mesh):
    in_specs = (
        P("req", "head", None),
        P(),
        P(None, None, "head"),
        P("head", None),
        P(None, None, "head"),
        P("req", None, None, None, "head"),
        P("req"),
        P("req", None),
        P("req", None),
        P(None, "req", "head", None, None),
        P("req", "head"),
        P("req", "head"),
        P("req", "head"),
        P("req", None),
    )
    out_specs = (P("req", "head", None), P(None, "req", "head", None, None))
    body = functools.partial(shards, reqs=mesh.shape["req"], heads=mesh.shape["head"])
    return jax.shard_map(body, mesh=mesh, in_specs=in_specs, out_specs=out_specs, check_vma=False)
```
